128 devices in a mesh: dp: 2 (over core), ctx: 16 (over z, y), tp: 4 (over x).
Axes of the slice: x: 4, y: 4, z: 4, core: 2. Of those that a mesh axis runs over, the one named last changes fastest.
Arguments:
- query: bfloat16 [8192, 32, 128], P(('dp', 'ctx'), 'tp'), parts along dimension 0, may hold values from -30 to 30
- keys: bfloat16 [8192, 4, 128], P(('dp', 'ctx'), 'tp'), parts along dimension 0, may hold values from -6 to 6
- values: bfloat16 [8192, 4, 128], P(('dp', 'ctx'), 'tp'), parts along dimension 0, may hold values from -6 to 6
- output_gradient: bfloat16 [8192, 32, 128], P(('dp', 'ctx'), 'tp'), parts along dimension 0, may hold values from -6 to 6
- doc_lengths: int32 [16], P('dp'), parts along dimension 0, may hold values from 1 to 2048, 4096 in all
- block_owner: int32 [32, 16], P('dp'), parts along dimension 0, may hold values from 0 to 15, each once within a row
Outputs:
- attended: bfloat16 [8192, 32, 128], P(('dp', 'ctx'), 'tp'), parts along dimension 0
- query_grad: bfloat16 [8192, 32, 128], P(('dp', 'ctx'), 'tp'), parts along dimension 0
- key_grad: bfloat16 [8192, 4, 128], P(('dp', 'ctx'), 'tp'), parts along dimension 0
- value_grad: bfloat16 [8192, 4, 128], P(('dp', 'ctx'), 'tp'), parts along dimension 0
The draws below stay inside these ranges and needn't reach their ends.
There are 2 independent parts, one for each index of `dp`. The reference program is written for one: setup_inputs(seed, part) draws one part's arguments, and reference() takes and returns one part's arrays. A program takes and returns all parts, laid end to end along the dimension named above; each array names one. Nothing has to cross between parts.
Inputs may be any that keep to these rules, and one draw needn't show every extreme that they name: `block_owner`: each row lists the owners of one loader shard's 16 blocks in order and names every owner once. `doc_lengths`: the lengths sum to 4096.
All inputs are finite; a program needn't handle non-finite values.
Results may differ from the reference program's by a relative error of at most 0.039.
Values may be sent and summed in bfloat16 or wider, within the bound.
A program may use at most 64 MiB of HBM per device.

```python
import math
import jax
import jax.numpy as jnp
import numpy as np
from jax import lax

QUERY_HEADS = 32
KEY_VALUE_HEADS = 4
HEAD_SIZE = 128
TOKENS_PER_OWNER = 256
NDOCS = 8
PACKED_TOKENS = 4096
N_CTX = 16


def draw_query(key, part):
    drawn_values = jnp.clip(jax.random.normal(jax.random.fold_in(key, 32), (PACKED_TOKENS, QUERY_HEADS, HEAD_SIZE), jnp.float32), -6.0, 6.0)
    return drawn_values.astype(jnp.bfloat16)


def draw_keys(key, part):
    drawn_values = jnp.clip(jax.random.normal(jax.random.fold_in(key, 42), (PACKED_TOKENS, KEY_VALUE_HEADS, HEAD_SIZE), jnp.float32), -6.0, 6.0)
    return drawn_values.astype(jnp.bfloat16)


def shard_levels(stream_key, shape, cuts, smallest, high):
    gain, own = 1.0, jax.random.fold_in(stream_key, 6)
    for dim, parts in cuts:
        steps = jnp.exp(jax.random.uniform(jax.random.fold_in(own, dim), (parts,), jnp.float32, smallest / len(cuts), high / len(cuts)))
        gain = gain * jnp.repeat(steps, shape[dim] // parts).reshape([-1 if axis == dim else 1 for axis in range(len(shape))])
    return gain


def length_profile(number_of, total, reach, slope):
    portions = [(1 << 20) // math.isqrt(rank ** slope) + 1 for rank in range(2, number_of + 1)]
    rest, given = total - reach - (number_of - 1), [1] * (number_of - 1)
    while rest > 0:
        movable = [i for i in range(number_of - 1) if given[i] < reach]
        pool, remaining = sum([portions[i] for i in movable]), rest
        for i in movable:
            extra = min(reach - given[i], max(1, remaining * portions[i] // pool), rest)
            given[i] = given[i] + extra
            rest = rest - extra
    return np.array([reach] + given)


def uneven(rng, number_of, total, limit, skew):
    if number_of == 2:
        one = jax.random.randint(rng, (), max(1, total - limit), min(limit, total - 1) + 1)
        return jnp.stack([one, total - one])
    tallies = jnp.asarray(length_profile(number_of, total, limit, skew), jnp.int32)
    pairs = (number_of - 1) // 2
    giver, taker = tallies[1:1 + 2 * pairs:2], tallies[2:2 + 2 * pairs:2]
    room = jnp.minimum(giver - 1, limit - taker)
    passed = jax.random.randint(jax.random.fold_in(rng, 1), (pairs,), 0, 1 << 20) % (room + 1)
    tallies = tallies.at[1:1 + 2 * pairs:2].set(giver - passed).at[2:2 + 2 * pairs:2].set(taker + passed)
    return tallies[jax.random.permutation(jax.random.fold_in(rng, 2), number_of)]


def gaussian(own_key, shape, scale, reach, cuts=(), kind=jnp.bfloat16):
    values = scale * jax.random.normal(own_key, shape, jnp.float32)
    if cuts:
        values = values * shard_levels(own_key, shape, cuts, -0.22, 0.18)
    return jnp.clip(values, -reach, reach).astype(kind)


def setup_inputs(seed: int = 0, part: int = 0) -> dict:
    arg_keys = jax.random.split(jax.random.key(seed), 7)
    own_keys = jax.random.split(jax.random.fold_in(arg_keys[6], part), 7)
    query = draw_query(jax.random.fold_in(jax.random.fold_in(arg_keys[6], part), 71), part)
    keys = draw_keys(jax.random.fold_in(jax.random.fold_in(arg_keys[6], part), 71), part)
    values = gaussian(own_keys[2], (PACKED_TOKENS, KEY_VALUE_HEADS, HEAD_SIZE), 1.0, 6.0, ((0, 16), (1, 4)))
    output_gradient = gaussian(own_keys[3], (PACKED_TOKENS, QUERY_HEADS, HEAD_SIZE), 1.0, 6.0, ((0, 16), (1, 4)))
    doc_lengths = uneven(own_keys[4], NDOCS, PACKED_TOKENS, PACKED_TOKENS // 2, 2).astype(jnp.int32)
    block_owner = jax.vmap(lambda own: jax.random.permutation(own, N_CTX))(jax.random.split(own_keys[5], N_CTX)).reshape((N_CTX, N_CTX)).astype(jnp.int32)
    return {"query": query, "keys": keys, "values": values, "output_gradient": output_gradient, "doc_lengths": doc_lengths, "block_owner": block_owner}


def document_index(token_positions, doc_lengths):
    doc_ends = jnp.cumsum(doc_lengths).astype(jnp.int32)
    return jnp.sum((doc_ends[None, :] <= token_positions[:, None]).astype(jnp.int32), axis=1)


def owner_positions(block_owner, owner_id, local_rows):
    cycle_size = block_owner.shape[0]
    block_rows = local_rows // cycle_size
    slot_ids = jnp.arange(cycle_size, dtype=jnp.int32)
    matches = (block_owner == owner_id).astype(jnp.int32)
    slot_of = jnp.sum(matches * slot_ids[None, :], axis=1)
    starts = slot_ids * local_rows + slot_of * block_rows
    return (starts[:, None] + jnp.arange(block_rows, dtype=jnp.int32)[None, :]).reshape(-1)


def rounded(source):
    narrow = source.astype(jnp.bfloat16)
    narrow = lax.optimization_barrier(narrow)
    return narrow.astype(jnp.float32)


def reference(query, keys, values, output_gradient, doc_lengths, block_owner):
    heads_per_group = QUERY_HEADS // KEY_VALUE_HEADS
    softmax_scale = HEAD_SIZE ** -0.5
    owner_ids = jnp.arange(N_CTX, dtype=jnp.int32)
    token_positions = jax.vmap(lambda owner_id: owner_positions(block_owner, owner_id, TOKENS_PER_OWNER))(owner_ids).reshape(-1)
    documents = document_index(token_positions, doc_lengths)
    query_rows_all = jnp.take(query, token_positions, axis=0).astype(jnp.float32).reshape(PACKED_TOKENS, KEY_VALUE_HEADS, heads_per_group, HEAD_SIZE)
    key_rows = jnp.take(keys, token_positions, axis=0).astype(jnp.float32)
    value_rows = jnp.take(values, token_positions, axis=0).astype(jnp.float32)
    output_gradients = jnp.take(output_gradient, token_positions, axis=0).astype(jnp.float32).reshape(PACKED_TOKENS, KEY_VALUE_HEADS, heads_per_group, HEAD_SIZE)

    def visible(query_pos, query_doc):
        allowed = (query_doc[:, None] == documents[None, :]) & (token_positions[None, :] <= query_pos[:, None])
        return allowed[:, None, None, :]

    query_block_list = query_rows_all.reshape(N_CTX, TOKENS_PER_OWNER, KEY_VALUE_HEADS, heads_per_group, HEAD_SIZE)
    gradient_blocks = output_gradients.reshape(N_CTX, TOKENS_PER_OWNER, KEY_VALUE_HEADS, heads_per_group, HEAD_SIZE)
    pos_blocks = token_positions.reshape(N_CTX, TOKENS_PER_OWNER)
    doc_blocks = documents.reshape(N_CTX, TOKENS_PER_OWNER)

    def forward_block(inputs):
        q_block, query_pos, query_doc = inputs
        allowed = visible(query_pos, query_doc)
        scores = jnp.einsum("tgrd,ugd->tgru", q_block, key_rows) * softmax_scale
        scores = jnp.where(allowed, scores, -jnp.inf)
        row_max = jnp.max(scores, axis=-1)
        weights = jnp.where(allowed, jnp.exp(scores - row_max[..., None]), 0.0)
        row_sum = jnp.sum(weights, axis=-1)
        mixed_rows = jnp.einsum("tgru,ugd->tgrd", rounded(weights), value_rows)
        attended = (mixed_rows / row_sum[..., None]).astype(jnp.bfloat16)
        return attended, row_max + jnp.log(row_sum)

    attended, log_sums = lax.map(forward_block, (query_block_list, pos_blocks, doc_blocks))
    attended_token_rows = attended.reshape(PACKED_TOKENS, KEY_VALUE_HEADS, heads_per_group, HEAD_SIZE)
    row_delta_sum = jnp.sum(output_gradients * attended_token_rows.astype(jnp.float32), axis=-1)

    def backward_block(accums, inputs):
        key_acc, value_acc = accums
        q_block, g_block, query_pos, query_doc, lse_block, delta_block = inputs
        allowed = visible(query_pos, query_doc)
        scores = jnp.einsum("tgrd,ugd->tgru", q_block, key_rows) * softmax_scale
        probs = jnp.where(allowed, jnp.exp(scores - lse_block[..., None]), 0.0)
        value_acc = value_acc + jnp.einsum("tgru,tgrd->ugd", rounded(probs), g_block)
        products = jnp.einsum("tgrd,ugd->tgru", g_block, value_rows)
        slopes = rounded(probs * (products - delta_block[..., None]))
        query_part = (jnp.einsum("tgru,ugd->tgrd", slopes, key_rows) * softmax_scale).astype(jnp.bfloat16)
        key_acc = key_acc + jnp.einsum("tgru,tgrd->ugd", slopes, q_block) * softmax_scale
        return (key_acc, value_acc), query_part

    empty_gradient_blocks = jnp.zeros((PACKED_TOKENS, KEY_VALUE_HEADS, HEAD_SIZE), jnp.float32)
    delta_block_list = row_delta_sum.reshape(N_CTX, TOKENS_PER_OWNER, KEY_VALUE_HEADS, heads_per_group)
    (key_acc, value_acc), query_grads = lax.scan(backward_block, (empty_gradient_blocks, empty_gradient_blocks), (query_block_list, gradient_blocks, pos_blocks, doc_blocks, log_sums, delta_block_list))
    return (attended_token_rows.reshape(PACKED_TOKENS, QUERY_HEADS, HEAD_SIZE), query_grads.reshape(PACKED_TOKENS, QUERY_HEADS, HEAD_SIZE), key_acc.astype(jnp.bfloat16), value_acc.astype(jnp.bfloat16))
```

```python
import functools

import jax
import jax.numpy as jnp
from jax import lax
from jax.experimental import pallas as pl
from jax.experimental.pallas import tpu as pltpu
from jax.sharding import PartitionSpec as P

NEG = -1e30
LOG2E = 1.4426950408889634
NT = (((1,), (1,)), ((), ()))
NN = (((1,), (0,)), ((), ()))


def dot(a, b, dims):
    return lax.dot_general(a, b, dims, preferred_element_type=jnp.float32)


def folded(x, op):
    return op(x.reshape(x.shape[0] // 8, 8, x.shape[1]), axis=0)


def attention_kernel(tile, scale, me, lengths, owners, q_ref, g_ref, kv_ref,
                     out_ref, dq_ref, dkv_ref,
                     kvt, acc, pair, s_buf, d_buf, o_acc, dq_acc):
    if me is None:
        me = lax.axis_index("ctx")
    shards, rows, width = q_ref.shape
    keys = kv_ref.shape[0]
    ndocs = lengths.shape[0]
    shard_rows = keys // shards
    block = shard_rows // shards
    heads = rows // block
    per_scale = scale * LOG2E

    acc[...] = jnp.zeros_like(acc)
    pair[...] = jnp.zeros_like(pair)

    @pl.loop(0, keys // 128)
    def _(b):
        at = pl.ds(pl.multiple_of(b * 128, 128), 128)
        kvt[0:width, at] = kv_ref[at, 0:width].T
        kvt[width:2 * width, at] = kv_ref[at, width:2 * width].T

    token = lax.broadcasted_iota(jnp.int32, (1, rows), 1) // heads
    key_index = lax.broadcasted_iota(jnp.int32, (tile, rows), 0)

    @pl.loop(0, shards)
    def _(j):
        slot = jnp.int32(0)
        for s in range(shards):
            slot = slot + jnp.where(owners[j, s] == me, s, 0)
        first = j * shard_rows + slot * block
        pos = first + token
        start = jnp.zeros_like(pos)
        low = jnp.int32(0)
        end = jnp.int32(0)
        for d in range(ndocs):
            end = end + lengths[d]
            start = jnp.where(end <= pos, end, start)
            low = jnp.where(end <= first, end, low)
        base = (low // 128) * 128
        count = (first + block - base + tile - 1) // tile

        pair[0:rows, 0:width] = q_ref[j]
        pair[rows:2 * rows, width:2 * width] = g_ref[j]

        def window(t):
            want = base + t * tile
            return want, pl.multiple_of(jnp.minimum(want, keys - tile), 128)

        def scores(t, peak):
            want, at = window(t)
            both = dot(kv_ref[pl.ds(at, tile), :], pair[...], NT)
            lower = jnp.maximum(start, want) - at
            allowed = (key_index >= lower) & (key_index <= pos - at)
            s = jnp.where(allowed, both[:, 0:rows], NEG)
            here = pl.ds(pl.multiple_of(t * tile, tile), tile)
            s_buf[here, :] = s
            d_buf[here, :] = both[:, rows:2 * rows]
            return jnp.maximum(peak, folded(s, jnp.max))

        peak = lax.fori_loop(0, count, scores, jnp.full((8, rows), NEG, jnp.float32))
        peak = jnp.max(peak, axis=0, keepdims=True)

        def weights(t, sums):
            here = pl.ds(pl.multiple_of(t * tile, tile), tile)
            p = jnp.exp2((s_buf[here, :] - peak) * per_scale)
            s_buf[here, :] = p
            return sums[0] + folded(p, jnp.sum), sums[1] + folded(p * d_buf[here, :], jnp.sum)

        zero = jnp.zeros((8, rows), jnp.float32)
        total, delta = lax.fori_loop(0, count, weights, (zero, zero))
        inverse = 1.0 / jnp.sum(total, axis=0, keepdims=True)
        delta = jnp.sum(delta, axis=0, keepdims=True) * inverse

        o_acc[...] = jnp.zeros_like(o_acc)
        dq_acc[...] = jnp.zeros_like(dq_acc)

        @pl.loop(0, count)
        def _(t):
            _, at = window(t)
            here = pl.ds(pl.multiple_of(t * tile, tile), tile)
            probs = s_buf[here, :] * inverse
            slopes = probs * (d_buf[here, :] - delta)
            probs = probs.astype(jnp.bfloat16)
            slopes = slopes.astype(jnp.bfloat16)
            span = pl.ds(at, tile)
            acc[span, :] += dot(jnp.concatenate([slopes, probs], axis=1), pair[...], NN)
            dq_acc[...] += dot(kvt[0:width, span], slopes, NN)
            o_acc[...] += dot(kvt[width:2 * width, span], probs, NN)

        out_ref[j] = o_acc[...].T.astype(jnp.bfloat16)
        dq_ref[j] = (dq_acc[...] * scale).T.astype(jnp.bfloat16)

    @pl.loop(0, shards)
    def _(j):
        for s in range(shards):
            rows_at = pl.ds(pl.multiple_of(j * shard_rows + s * block, block), block)
            part = acc[rows_at, :]
            owner = owners[j, s]
            dkv_ref[owner, j, :, 0:width] = (part[:, 0:width] * scale).astype(jnp.bfloat16)
            dkv_ref[owner, j, :, width:2 * width] = part[:, width:2 * width].astype(jnp.bfloat16)


def attention(q, g, kv, lengths, owners, me=None, tile=512, interpret=False):
    shards, rows, width = q.shape
    keys = kv.shape[0]
    block = keys // shards // shards
    reach = -(-(2048 + block + 128) // tile) * tile
    smem = pl.BlockSpec(memory_space=pltpu.SMEM)
    vmem = pl.BlockSpec(memory_space=pltpu.VMEM)
    return pl.pallas_call(
        functools.partial(attention_kernel, tile, width ** -0.5, me),
        out_shape=(
            jax.ShapeDtypeStruct((shards, rows, width), jnp.bfloat16),
            jax.ShapeDtypeStruct((shards, rows, width), jnp.bfloat16),
            jax.ShapeDtypeStruct((shards, shards, block, 2 * width), jnp.bfloat16),
        ),
        in_specs=[smem, smem, vmem, vmem, vmem],
        out_specs=(vmem, vmem, vmem),
        scratch_shapes=[
            pltpu.VMEM((2 * width, keys), jnp.bfloat16),
            pltpu.VMEM((keys, 2 * width), jnp.float32),
            pltpu.VMEM((2 * rows, 2 * width), jnp.bfloat16),
            pltpu.VMEM((reach, rows), jnp.float32),
            pltpu.VMEM((reach, rows), jnp.float32),
            pltpu.VMEM((width, rows), jnp.float32),
            pltpu.VMEM((width, rows), jnp.float32),
        ],
        compiler_params=pltpu.CompilerParams(vmem_limit_bytes=40 << 20),
        interpret=interpret,
    )(lengths, owners, q, g, kv)


def on_device(query, keys, values, output_gradient, doc_lengths, block_owner):
    shards = lax.axis_size("ctx")
    me = lax.axis_index("ctx")
    local, heads, width = query.shape
    block = local // shards
    targets = lax.dynamic_index_in_dim(block_owner, me, 0, keepdims=False)
    ids = jnp.arange(shards, dtype=jnp.int32)
    order = jnp.sum((targets[:, None] == ids[None, :]).astype(jnp.int32) * ids[:, None], axis=0)

    def arrange(source):
        moved = jnp.take(source.reshape(shards, block * heads, width), order, axis=0)
        return lax.all_to_all(moved, "ctx", split_axis=0, concat_axis=0, tiled=True)

    kv = lax.all_gather(jnp.concatenate([keys[:, 0], values[:, 0]], axis=1), "ctx", tiled=True)
    out, dq, dkv = attention(arrange(query), arrange(output_gradient), kv, doc_lengths, block_owner)
    dkv = lax.psum_scatter(dkv, "ctx", scatter_dimension=0, tiled=True).reshape(local, 2 * width)
    return (
        out.reshape(local, heads, width),
        dq.reshape(local, heads, width),
        dkv[:, None, :width],
        dkv[:, None, width:],
    )


def solution(mesh):
    rows = P(("dp", "ctx"), "tp", None)
    return jax.shard_map(
        on_device,
        mesh=mesh,
        in_specs=(rows, rows, rows, rows, P("dp"), P("dp", None)),
        out_specs=(rows, rows, rows, rows),
        check_vma=False,
    )
```

```python
import functools

import jax
import jax.numpy as jnp
from jax import lax
from jax.experimental import pallas as pl
from jax.experimental.pallas import tpu as pltpu
from jax.sharding import PartitionSpec as P

NEG = -1e30
LOG2E = 1.4426950408889634
NT = (((1,), (1,)), ((), ()))
NN = (((1,), (0,)), ((), ()))


def dot(a, b, dims):
    return lax.dot_general(a, b, dims, preferred_element_type=jnp.float32)


def folded(x, op):
    return op(x.reshape(x.shape[0] // 8, 8, x.shape[1]), axis=0)


SIDE = 4
MESH_AXIS = "ctx"


def coordinates():
    me = lax.axis_index(MESH_AXIS)
    return lax.div(me, SIDE), lax.rem(me, SIDE)


def device_at(dz, dy):
    z, y = coordinates()
    return lax.rem(z + dz + SIDE, SIDE) * SIDE + lax.rem(y + dy + SIDE, SIDE)


def greet(offsets):
    barrier = pltpu.get_barrier_semaphore()
    for dz, dy in offsets:
        pl.semaphore_signal(barrier, inc=1, device_id={MESH_AXIS: device_at(dz, dy)},
                            device_id_type=pl.DeviceIdType.MESH)
    pl.semaphore_wait(barrier, len(offsets))


class Copies:
    def __init__(self, send_sems, recv_sems):
        self.send_sems, self.recv_sems, self.sent = send_sems, recv_sems, []

    def make(self, n, src, dst, target):
        return pltpu.make_async_remote_copy(
            src_ref=src, dst_ref=dst, send_sem=self.send_sems.at[n], recv_sem=self.recv_sems.at[n],
            device_id={MESH_AXIS: target}, device_id_type=pl.DeviceIdType.MESH)

    def send(self, n, src, dst, target):
        copy = self.make(n, src, dst, target)
        copy.start()
        self.sent.append(copy)

    def arrived(self, n, dst):
        self.make(n, dst, dst, device_at(0, 1)).wait_recv()

    def finish(self):
        for copy in self.sent:
            copy.wait_send()


OFFSETS = [(dz, dy) for dz in (0, 1, 2, 3) for dy in (0, 1, 2, 3) if (dz, dy) != (0, 0)]


class Spread:
    def __init__(self, first_is_y, own, blocks, copies, base):
        self.first_is_y, self.own, self.blocks, self.copies, self.base = first_is_y, own, blocks, copies, base
        self.half = blocks.shape[1] // 2

    def block(self, a, b):
        return device_at(b, a) if self.first_is_y else device_at(a, b)

    def part(self, a, b, half):
        block = self.blocks.at[self.block(a, b)]
        return block if half is None else block.at[pl.ds(half * self.half, self.half)]

    def number(self, stage, a, kind):
        return self.base + (kind if stage == 1 else 4 + 4 * (a % SIDE) + kind)

    def send(self, stage, a, kind, src, part):
        step = 1 if kind in (0, 2) else -1
        target = self.block(step, 0) if stage == 1 else self.block(0, step)
        self.copies.send(self.number(stage, a, kind), src, part, target)

    def start(self):
        me = self.part(0, 0, None)
        for stage in (1, 2):
            for kind in (0, 1):
                self.send(stage, 0, kind, self.own, me)

    def got(self, stage, a, kind):
        along = {0: -1, 1: 1, 2: 2, 3: 2}[kind]
        half = {0: None, 1: None, 2: 0, 3: 1}[kind]
        part = self.part(along, 0, half) if stage == 1 else self.part(a, along, half)
        self.copies.arrived(self.number(stage, a, kind), part)

    def onward(self, stage, a, kind):
        along = -1 if kind == 0 else 1
        half = kind
        part = self.part(along, 0, half) if stage == 1 else self.part(a, along, half)
        self.send(stage, a, kind + 2, part, part)

    def second(self, a):
        part = self.part(a, 0, None)
        for kind in (0, 1):
            self.send(2, a, kind, part, part)


def exchange_kernel(owners, q_ref, g_ref, k_ref, v_ref, qg_out, k_out, v_out,
                    staging, send_sems, recv_sems):
    me = lax.axis_index(MESH_AXIS)
    rows = q_ref.shape[1]
    copies = Copies(send_sems, recv_sems)
    k_spread = Spread(True, k_ref, k_out, copies, 0)
    v_spread = Spread(False, v_ref, v_out, copies, 20)
    spreads = (k_spread, v_spread)

    greet(OFFSETS)
    for spread in spreads:
        spread.start()
    k_out[me] = k_ref[...]
    v_out[me] = v_ref[...]

    def slot_for(target):
        slot = jnp.int32(0)
        for s in range(SIDE * SIDE):
            slot = jnp.where(owners[me, s] == target, s, slot)
        return slot

    def reassign(items):
        for n in items:
            target = device_at(*OFFSETS[n])
            slot = slot_for(target)
            staging[n, 0:rows] = q_ref[slot]
            staging[n, rows:2 * rows] = g_ref[slot]
            copies.send(40 + n, staging.at[n], qg_out.at[me], target)

    far = sorted(range(15), key=lambda n: -sum(min(d, SIDE - d) for d in OFFSETS[n]))
    reassign(far[:5])
    for kind in (0, 1):
        for spread in spreads:
            spread.got(1, 0, kind)
            spread.onward(1, 0, kind)
            spread.second(-1 if kind == 0 else 1)
    reassign(far[5:10])
    for spread in spreads:
        spread.got(1, 0, 2)
        spread.got(1, 0, 3)
        spread.second(2)
    for kind in (0, 1):
        for spread in spreads:
            spread.got(2, 0, kind)
            spread.onward(2, 0, kind)
    reassign(far[10:])
    slot = slot_for(me)
    qg_out[me, 0:rows] = q_ref[slot]
    qg_out[me, rows:2 * rows] = g_ref[slot]
    for a in (-1, 1, 2):
        for kind in (0, 1):
            for spread in spreads:
                spread.got(2, a, kind)
                spread.onward(2, a, kind)
    for a in (0, -1, 1, 2):
        for kind in (2, 3):
            for spread in spreads:
                spread.got(2, a, kind)
    for n in far:
        dz, dy = OFFSETS[n]
        copies.arrived(40 + n, qg_out.at[device_at(-dz, -dy)])
    copies.finish()


def exchange(owners, q, g, k, v):
    shards, rows, width = q.shape
    local = k.shape[0]
    smem = pl.BlockSpec(memory_space=pltpu.SMEM)
    vmem = pl.BlockSpec(memory_space=pltpu.VMEM)
    bf16 = jnp.bfloat16
    return pl.pallas_call(
        exchange_kernel,
        out_shape=(
            jax.ShapeDtypeStruct((shards, 2 * rows, width), bf16),
            jax.ShapeDtypeStruct((shards, local, width), bf16),
            jax.ShapeDtypeStruct((shards, local, width), bf16),
        ),
        in_specs=[smem, vmem, vmem, vmem, vmem],
        out_specs=(vmem, vmem, vmem),
        scratch_shapes=[
            pltpu.VMEM((shards - 1, 2 * rows, width), bf16),
            pltpu.SemaphoreType.DMA((55,)),
            pltpu.SemaphoreType.DMA((55,)),
        ],
        compiler_params=pltpu.CompilerParams(
            collective_id=0, has_side_effects=True, vmem_limit_bytes=24 << 20),
    )(owners, q, g, k, v)


class Collect:
    PLUS, MINUS = (2, 0), (1, 3)

    def __init__(self, first_is_y, blocks, out, copies, base, passing, joined, left, right,
                 sums, own_sum, passing2, joined2, left2, right2):
        self.first_is_y, self.blocks, self.out, self.copies, self.base = first_is_y, blocks, out, copies, base
        self.passing, self.joined, self.left, self.right = passing, joined, left, right
        self.sums, self.own_sum = sums, own_sum
        self.passing2, self.joined2, self.left2, self.right2 = passing2, joined2, left2, right2
        self.half = out.shape[0] // 2

    def device(self, a, b):
        return device_at(b, a) if self.first_is_y else device_at(a, b)

    def begin(self):
        for b in (2, 1, 0, 3):
            step = 1 if b in self.PLUS else -1
            self.copies.send(self.base + b, self.blocks.at[self.device(2, b)], self.passing.at[b],
                             self.device(step, 0))
        for b in (2, 1, 3, 0):
            if b in self.PLUS:
                self.copies.send(self.base + 8 + b, self.blocks.at[self.device(-1, b)],
                                 self.right.at[b], self.device(-1, 0))
            else:
                self.copies.send(self.base + 4 + b, self.blocks.at[self.device(1, b)],
                                 self.left.at[b], self.device(1, 0))

    def join(self, b):
        self.copies.arrived(self.base + b, self.passing.at[b])
        step = 1 if b in self.PLUS else -1
        mine = self.blocks[self.device(step, b)].astype(jnp.float32)
        self.joined[b] = (mine + self.passing[b].astype(jnp.float32)).astype(jnp.bfloat16)
        if step == 1:
            self.copies.send(self.base + 4 + b, self.joined.at[b], self.left.at[b], self.device(1, 0))
        else:
            self.copies.send(self.base + 8 + b, self.joined.at[b], self.right.at[b], self.device(-1, 0))

    def total(self, b):
        self.copies.arrived(self.base + 4 + b, self.left.at[b])
        self.copies.arrived(self.base + 8 + b, self.right.at[b])
        total = (self.blocks[self.device(0, b)].astype(jnp.float32)
                 + self.left[b].astype(jnp.float32) + self.right[b].astype(jnp.float32))
        if b == 0:
            self.own_sum[...] = total
        else:
            self.sums[b] = total.astype(jnp.bfloat16)

    def rows(self, half):
        return pl.ds(half * self.half, self.half)

    def begin2(self, b):
        if b == 2:
            for half in (0, 1):
                self.copies.send(self.base + 12 + half, self.sums.at[2, self.rows(half)],
                                 self.passing2.at[half], self.device(0, 1 - 2 * half))
        elif b == 1:
            self.copies.send(self.base + 14, self.sums.at[1, self.rows(1)],
                             self.left2.at[self.rows(1)], self.device(0, 1))
        else:
            self.copies.send(self.base + 15, self.sums.at[3, self.rows(0)],
                             self.right2.at[self.rows(0)], self.device(0, -1))

    def join2(self, half):
        self.copies.arrived(self.base + 12 + half, self.passing2.at[half])
        b = 1 if half == 0 else 3
        mine = self.sums[b, self.rows(half)].astype(jnp.float32)
        self.joined2[half] = (mine + self.passing2[half].astype(jnp.float32)).astype(jnp.bfloat16)
        if half == 0:
            self.copies.send(self.base + 16, self.joined2.at[0], self.left2.at[self.rows(0)],
                             self.device(0, 1))
        else:
            self.copies.send(self.base + 17, self.joined2.at[1], self.right2.at[self.rows(1)],
                             self.device(0, -1))

    def end(self):
        self.copies.arrived(self.base + 14, self.left2.at[self.rows(1)])
        self.copies.arrived(self.base + 15, self.right2.at[self.rows(0)])
        self.copies.arrived(self.base + 16, self.left2.at[self.rows(0)])
        self.copies.arrived(self.base + 17, self.right2.at[self.rows(1)])
        total = self.own_sum[...] + self.left2[...].astype(jnp.float32) + self.right2[...].astype(jnp.float32)
        self.out[...] = total.astype(jnp.bfloat16)


def collect_kernel(dk_ref, dv_ref, dk_out, dv_out, passing, joined, left, right, sums, own_sum,
                   passing2, joined2, left2, right2, send_sems, recv_sems):
    copies = Copies(send_sems, recv_sems)
    k_sum, v_sum = [
        Collect(i == 0, blocks, out, copies, 18 * i, passing.at[i], joined.at[i], left.at[i], right.at[i],
                sums.at[i], own_sum.at[i], passing2.at[i], joined2.at[i], left2.at[i], right2.at[i])
        for i, (blocks, out) in enumerate(((dk_ref, dk_out), (dv_ref, dv_out)))]
    both = (k_sum, v_sum)
    greet([(1, 0), (3, 0), (0, 1), (0, 3)])
    for one in both:
        one.begin()
    for b in (2, 1, 0, 3):
        for one in both:
            one.join(b)
    for b in (2, 1, 3):
        for one in both:
            one.total(b)
            one.begin2(b)
    for half in (0, 1):
        for one in both:
            one.join2(half)
    for one in both:
        one.total(0)
    for one in both:
        one.end()
    copies.finish()


def collect(dk, dv):
    shards, local, width = dk.shape
    bf16 = jnp.bfloat16
    vmem = pl.BlockSpec(memory_space=pltpu.VMEM)
    full = (2, SIDE, local, width)
    return pl.pallas_call(
        collect_kernel,
        out_shape=(jax.ShapeDtypeStruct((local, width), bf16),) * 2,
        in_specs=[vmem, vmem],
        out_specs=(vmem, vmem),
        scratch_shapes=[
            pltpu.VMEM(full, bf16), pltpu.VMEM(full, bf16), pltpu.VMEM(full, bf16), pltpu.VMEM(full, bf16),
            pltpu.VMEM(full, bf16), pltpu.VMEM((2, local, width), jnp.float32),
            pltpu.VMEM((2, 2, local // 2, width), bf16), pltpu.VMEM((2, 2, local // 2, width), bf16),
            pltpu.VMEM((2, local, width), bf16), pltpu.VMEM((2, local, width), bf16),
            pltpu.SemaphoreType.DMA((36,)),
            pltpu.SemaphoreType.DMA((36,)),
        ],
        compiler_params=pltpu.CompilerParams(
            collective_id=1, has_side_effects=True, vmem_limit_bytes=24 << 20),
    )(dk, dv)


def attention_kernel(tile, scale, me, lengths, owners, qg_ref, k_ref, v_ref,
                     out_ref, dq_ref, dk_ref, dv_ref,
                     kvt, acc, pair, s_buf, d_buf, o_acc, dq_acc):
    if me is None:
        me = lax.axis_index("ctx")
    shards, rows, width = qg_ref.shape
    rows = rows // 2
    keys = k_ref.shape[0]
    ndocs = lengths.shape[0]
    shard_rows = keys // shards
    block = shard_rows // shards
    heads = rows // block
    per_scale = scale * LOG2E

    acc[...] = jnp.zeros_like(acc)
    pair[...] = jnp.zeros_like(pair)

    @pl.loop(0, keys // 128)
    def _(b):
        at = pl.ds(pl.multiple_of(b * 128, 128), 128)
        kvt[0:width, at] = k_ref[at, :].T
        kvt[width:2 * width, at] = v_ref[at, :].T

    token = lax.broadcasted_iota(jnp.int32, (1, rows), 1) // heads
    key_index = lax.broadcasted_iota(jnp.int32, (tile, rows), 0)

    @pl.loop(0, shards)
    def _(j):
        slot = jnp.int32(0)
        for s in range(shards):
            slot = jnp.where(owners[j, s] == me, s, slot)
        first = j * shard_rows + slot * block
        pos = first + token
        start = jnp.zeros_like(pos)
        low = jnp.int32(0)
        end = jnp.int32(0)
        for d in range(ndocs):
            end = end + lengths[d]
            start = jnp.where(end <= pos, end, start)
            low = jnp.where(end <= first, end, low)
        base = (low // 128) * 128
        count = (first + block - base + tile - 1) // tile

        pair[0:rows, 0:width] = qg_ref[j, 0:rows]
        pair[rows:2 * rows, width:2 * width] = qg_ref[j, rows:2 * rows]

        def window(t):
            want = base + t * tile
            return want, pl.multiple_of(jnp.minimum(want, keys - tile), 128)

        def scores(t, peak):
            want, at = window(t)
            span = pl.ds(at, tile)
            both = dot(jnp.concatenate([k_ref[span, :], v_ref[span, :]], axis=1), pair[...], NT)
            lower = jnp.maximum(start, want) - at
            allowed = (key_index >= lower) & (key_index <= pos - at)
            s = jnp.where(allowed, both[:, 0:rows], NEG)
            here = pl.ds(pl.multiple_of(t * tile, tile), tile)
            s_buf[here, :] = s
            d_buf[here, :] = both[:, rows:2 * rows]
            return jnp.maximum(peak, folded(s, jnp.max))

        peak = lax.fori_loop(0, count, scores, jnp.full((8, rows), NEG, jnp.float32))
        peak = jnp.max(peak, axis=0, keepdims=True)

        def weights(t, sums):
            here = pl.ds(pl.multiple_of(t * tile, tile), tile)
            p = jnp.exp2((s_buf[here, :] - peak) * per_scale)
            s_buf[here, :] = p
            return sums[0] + folded(p, jnp.sum), sums[1] + folded(p * d_buf[here, :], jnp.sum)

        zero = jnp.zeros((8, rows), jnp.float32)
        total, delta = lax.fori_loop(0, count, weights, (zero, zero))
        inverse = 1.0 / jnp.sum(total, axis=0, keepdims=True)
        delta = jnp.sum(delta, axis=0, keepdims=True) * inverse

        o_acc[...] = jnp.zeros_like(o_acc)
        dq_acc[...] = jnp.zeros_like(dq_acc)

        @pl.loop(0, count)
        def _(t):
            _, at = window(t)
            here = pl.ds(pl.multiple_of(t * tile, tile), tile)
            probs = s_buf[here, :] * inverse
            slopes = probs * (d_buf[here, :] - delta)
            probs = probs.astype(jnp.bfloat16)
            slopes = slopes.astype(jnp.bfloat16)
            span = pl.ds(at, tile)
            acc[span, :] += dot(jnp.concatenate([slopes, probs], axis=1), pair[...], NN)
            dq_acc[...] += dot(kvt[0:width, span], slopes, NN)
            o_acc[...] += dot(kvt[width:2 * width, span], probs, NN)

        out_ref[j] = o_acc[...].T.astype(jnp.bfloat16)
        dq_ref[j] = (dq_acc[...] * scale).T.astype(jnp.bfloat16)

    @pl.loop(0, shards)
    def _(j):
        for s in range(shards):
            rows_at = pl.ds(pl.multiple_of(j * shard_rows + s * block, block), block)
            part = acc[rows_at, :]
            owner = owners[j, s]
            dk_ref[owner, j] = (part[:, 0:width] * scale).astype(jnp.bfloat16)
            dv_ref[owner, j] = part[:, width:2 * width].astype(jnp.bfloat16)


def attention(qg, k, v, lengths, owners, me=None, tile=512, interpret=False):
    shards, rows, width = qg.shape
    rows = rows // 2
    local = k.shape[1]
    keys = shards * local
    block = keys // shards // shards
    reach = -(-(2048 + block + 128) // tile) * tile
    smem = pl.BlockSpec(memory_space=pltpu.SMEM)
    vmem = pl.BlockSpec(memory_space=pltpu.VMEM)
    out, dq, dk, dv = pl.pallas_call(
        functools.partial(attention_kernel, tile, width ** -0.5, me),
        out_shape=(
            jax.ShapeDtypeStruct((shards, rows, width), jnp.bfloat16),
            jax.ShapeDtypeStruct((shards, rows, width), jnp.bfloat16),
            jax.ShapeDtypeStruct((shards, shards, block, width), jnp.bfloat16),
            jax.ShapeDtypeStruct((shards, shards, block, width), jnp.bfloat16),
        ),
        in_specs=[smem, smem, vmem, vmem, vmem],
        out_specs=(vmem, vmem, vmem, vmem),
        scratch_shapes=[
            pltpu.VMEM((2 * width, keys), jnp.bfloat16),
            pltpu.VMEM((keys, 2 * width), jnp.float32),
            pltpu.VMEM((2 * rows, 2 * width), jnp.bfloat16),
            pltpu.VMEM((reach, rows), jnp.float32),
            pltpu.VMEM((reach, rows), jnp.float32),
            pltpu.VMEM((width, rows), jnp.float32),
            pltpu.VMEM((width, rows), jnp.float32),
        ],
        compiler_params=pltpu.CompilerParams(vmem_limit_bytes=40 << 20),
        interpret=interpret,
    )(lengths, owners, qg, k.reshape(keys, width), v.reshape(keys, width))
    return out, dq, dk.reshape(shards, local, width), dv.reshape(shards, local, width)


def on_device(query, keys, values, output_gradient, doc_lengths, block_owner):
    local, heads, width = query.shape
    shards = SIDE * SIDE
    rows = local // shards * heads
    qg, k, v = exchange(block_owner, query.reshape(shards, rows, width),
                        output_gradient.reshape(shards, rows, width), keys[:, 0], values[:, 0])
    out, dq, dk, dv = attention(qg, k, v, doc_lengths, block_owner)
    dk, dv = collect(dk, dv)
    return (
        out.reshape(local, heads, width),
        dq.reshape(local, heads, width),
        dk[:, None],
        dv[:, None],
    )


def solution(mesh):
    rows = P(("dp", "ctx"), "tp", None)
    return jax.shard_map(
        on_device,
        mesh=mesh,
        in_specs=(rows, rows, rows, rows, P("dp"), P("dp", None)),
        out_specs=(rows, rows, rows, rows),
        check_vma=False,
    )
```

```python
import functools

import jax
import jax.numpy as jnp
from jax import lax
from jax.experimental import pallas as pl
from jax.experimental.pallas import tpu as pltpu
from jax.sharding import PartitionSpec as P

NEG = -1e30
LOG2E = 1.4426950408889634
NT = (((1,), (1,)), ((), ()))
NN = (((1,), (0,)), ((), ()))


def dot(a, b, dims):
    return lax.dot_general(a, b, dims, preferred_element_type=jnp.float32)


def folded(x, op):
    return op(x.reshape(x.shape[0] // 8, 8, x.shape[1]), axis=0)


SIDE = 4
MESH_AXIS = "ctx"


def coordinates():
    me = lax.axis_index(MESH_AXIS)
    return lax.div(me, SIDE), lax.rem(me, SIDE)


def device_at(dz, dy):
    z, y = coordinates()
    return lax.rem(z + dz + SIDE, SIDE) * SIDE + lax.rem(y + dy + SIDE, SIDE)


def greet(offsets):
    barrier = pltpu.get_barrier_semaphore()
    for dz, dy in offsets:
        pl.semaphore_signal(barrier, inc=1, device_id={MESH_AXIS: device_at(dz, dy)},
                            device_id_type=pl.DeviceIdType.MESH)
    pl.semaphore_wait(barrier, len(offsets))


class Copies:
    def __init__(self, send_sems, recv_sems):
        self.send_sems, self.recv_sems, self.sent = send_sems, recv_sems, []

    def make(self, n, src, dst, target):
        return pltpu.make_async_remote_copy(
            src_ref=src, dst_ref=dst, send_sem=self.send_sems.at[n], recv_sem=self.recv_sems.at[n],
            device_id={MESH_AXIS: target}, device_id_type=pl.DeviceIdType.MESH)

    def send(self, n, src, dst, target):
        copy = self.make(n, src, dst, target)
        copy.start()
        self.sent.append(copy)

    def arrived(self, n, dst):
        self.make(n, dst, dst, device_at(0, 1)).wait_recv()

    def finish(self):
        for copy in self.sent:
            copy.wait_send()


OFFSETS = [(dz, dy) for dz in (0, 1, 2, 3) for dy in (0, 1, 2, 3) if (dz, dy) != (0, 0)]


class Spread:
    def __init__(self, first_is_y, own, blocks, copies, base):
        self.first_is_y, self.own, self.blocks, self.copies, self.base = first_is_y, own, blocks, copies, base
        self.half = blocks.shape[1] // 2

    def block(self, a, b):
        return device_at(b, a) if self.first_is_y else device_at(a, b)

    def part(self, a, b, half):
        block = self.blocks.at[self.block(a, b)]
        return block if half is None else block.at[pl.ds(half * self.half, self.half)]

    def number(self, stage, a, kind):
        return self.base + (kind if stage == 1 else 4 + 4 * (a % SIDE) + kind)

    def send(self, stage, a, kind, src, part):
        step = 1 if kind in (0, 2) else -1
        target = self.block(step, 0) if stage == 1 else self.block(0, step)
        self.copies.send(self.number(stage, a, kind), src, part, target)

    def start(self):
        me = self.part(0, 0, None)
        for stage in (1, 2):
            for kind in (0, 1):
                self.send(stage, 0, kind, self.own, me)

    def got(self, stage, a, kind):
        along = {0: -1, 1: 1, 2: 2, 3: 2}[kind]
        half = {0: None, 1: None, 2: 0, 3: 1}[kind]
        part = self.part(along, 0, half) if stage == 1 else self.part(a, along, half)
        self.copies.arrived(self.number(stage, a, kind), part)

    def onward(self, stage, a, kind):
        along = -1 if kind == 0 else 1
        half = kind
        part = self.part(along, 0, half) if stage == 1 else self.part(a, along, half)
        self.send(stage, a, kind + 2, part, part)

    def second(self, a):
        part = self.part(a, 0, None)
        for kind in (0, 1):
            self.send(2, a, kind, part, part)


def exchange_kernel(owners, q_hbm, g_hbm, k_hbm, v_hbm, qg_out, k_out, v_out, kvt,
                    q_in, g_in, staging, load_sems, send_sems, recv_sems):
    me = lax.axis_index(MESH_AXIS)
    width = k_out.shape[2]
    loads = [pltpu.make_async_copy(src, dst, load_sems.at[n]) for n, (src, dst) in enumerate((
        (k_hbm, k_out.at[me]), (v_hbm, v_out.at[me]), (q_hbm, q_in), (g_hbm, g_in)))]
    for load in loads:
        load.start()
    copies = Copies(send_sems, recv_sems)
    spreads = (Spread(True, k_out.at[me], k_out, copies, 0), Spread(False, v_out.at[me], v_out, copies, 20))
    greet(OFFSETS)
    loads[0].wait()
    loads[1].wait()
    for spread in spreads:
        spread.start()
    loads[2].wait()
    loads[3].wait()

    def slot_for(target):
        slot = jnp.int32(0)
        for s in range(SIDE * SIDE):
            slot = jnp.where(owners[me, s] == target, s, slot)
        return slot

    def reassign(items):
        for n in items:
            target = device_at(*OFFSETS[n])
            slot = slot_for(target)
            staging[n, 0] = q_in[slot]
            staging[n, 1] = g_in[slot]
            copies.send(40 + n, staging.at[n], qg_out.at[:, me], target)

    far = sorted(range(15), key=lambda n: -sum(min(d, SIDE - d) for d in OFFSETS[n]))
    reassign(far[:5])
    for kind in (0, 1):
        for spread in spreads:
            spread.got(1, 0, kind)
            spread.onward(1, 0, kind)
            spread.second(-1 if kind == 0 else 1)
    reassign(far[5:10])
    for spread in spreads:
        spread.got(1, 0, 2)
        spread.got(1, 0, 3)
        spread.second(2)
    for kind in (0, 1):
        for spread in spreads:
            spread.got(2, 0, kind)
            spread.onward(2, 0, kind)
    reassign(far[10:])
    slot = slot_for(me)
    qg_out[0, me] = q_in[slot]
    qg_out[1, me] = g_in[slot]
    for a in (-1, 1, 2):
        for kind in (0, 1):
            for spread in spreads:
                spread.got(2, a, kind)
                spread.onward(2, a, kind)
    for a in (0, -1, 1, 2):
        for kind in (2, 3):
            for spread in spreads:
                spread.got(2, a, kind)

    @pl.loop(0, SIDE * SIDE)
    def _(b):
        for h in range(k_out.shape[1] // 128):
            at = pl.ds(pl.multiple_of(b * k_out.shape[1] + h * 128, 128), 128)
            kvt[0:width, at] = k_out[b, h * 128:(h + 1) * 128].T
            kvt[width:2 * width, at] = v_out[b, h * 128:(h + 1) * 128].T

    for n in far:
        dz, dy = OFFSETS[n]
        copies.arrived(40 + n, qg_out.at[:, device_at(-dz, -dy)])
    copies.finish()


def exchange(owners, q, g, k, v):
    shards, rows, width = q.shape
    local = k.shape[0]
    smem = pl.BlockSpec(memory_space=pltpu.SMEM)
    vmem = pl.BlockSpec(memory_space=pltpu.VMEM)
    hbm = pl.BlockSpec(memory_space=pltpu.HBM)
    bf16 = jnp.bfloat16
    return pl.pallas_call(
        exchange_kernel,
        out_shape=(
            jax.ShapeDtypeStruct((2, shards, rows, width), bf16),
            jax.ShapeDtypeStruct((shards, local, width), bf16),
            jax.ShapeDtypeStruct((shards, local, width), bf16),
            jax.ShapeDtypeStruct((2 * width, shards * local), bf16),
        ),
        in_specs=[smem, hbm, hbm, hbm, hbm],
        out_specs=(vmem, vmem, vmem, vmem),
        scratch_shapes=[
            pltpu.VMEM((shards, rows, width), bf16),
            pltpu.VMEM((shards, rows, width), bf16),
            pltpu.VMEM((shards - 1, 2, rows, width), bf16),
            pltpu.SemaphoreType.DMA((4,)),
            pltpu.SemaphoreType.DMA((55,)),
            pltpu.SemaphoreType.DMA((55,)),
        ],
        compiler_params=pltpu.CompilerParams(
            collective_id=0, has_side_effects=True, vmem_limit_bytes=24 << 20),
    )(owners, q, g, k, v)


class Collect:
    PLUS, MINUS = (2, 0), (1, 3)

    def __init__(self, first_is_y, blocks, out, copies, base, passing, joined, left, right,
                 sums, own_sum, passing2, joined2, left2, right2):
        self.first_is_y, self.blocks, self.out, self.copies, self.base = first_is_y, blocks, out, copies, base
        self.passing, self.joined, self.left, self.right = passing, joined, left, right
        self.sums, self.own_sum = sums, own_sum
        self.passing2, self.joined2, self.left2, self.right2 = passing2, joined2, left2, right2
        self.half = out.shape[0] // 2

    def device(self, a, b):
        return device_at(b, a) if self.first_is_y else device_at(a, b)

    def begin(self):
        for b in (2, 1, 0, 3):
            step = 1 if b in self.PLUS else -1
            self.copies.send(self.base + b, self.blocks.at[self.device(2, b)], self.passing.at[b],
                             self.device(step, 0))
        for b in (2, 1, 3, 0):
            if b in self.PLUS:
                self.copies.send(self.base + 8 + b, self.blocks.at[self.device(-1, b)],
                                 self.right.at[b], self.device(-1, 0))
            else:
                self.copies.send(self.base + 4 + b, self.blocks.at[self.device(1, b)],
                                 self.left.at[b], self.device(1, 0))

    def join(self, b):
        self.copies.arrived(self.base + b, self.passing.at[b])
        step = 1 if b in self.PLUS else -1
        mine = self.blocks[self.device(step, b)].astype(jnp.float32)
        self.joined[b] = (mine + self.passing[b].astype(jnp.float32)).astype(jnp.bfloat16)
        if step == 1:
            self.copies.send(self.base + 4 + b, self.joined.at[b], self.left.at[b], self.device(1, 0))
        else:
            self.copies.send(self.base + 8 + b, self.joined.at[b], self.right.at[b], self.device(-1, 0))

    def total(self, b):
        self.copies.arrived(self.base + 4 + b, self.left.at[b])
        self.copies.arrived(self.base + 8 + b, self.right.at[b])
        total = (self.blocks[self.device(0, b)].astype(jnp.float32)
                 + self.left[b].astype(jnp.float32) + self.right[b].astype(jnp.float32))
        if b == 0:
            self.own_sum[...] = total
        else:
            self.sums[b] = total.astype(jnp.bfloat16)

    def rows(self, half):
        return pl.ds(half * self.half, self.half)

    def begin2(self, b):
        if b == 2:
            for half in (0, 1):
                self.copies.send(self.base + 12 + half, self.sums.at[2, self.rows(half)],
                                 self.passing2.at[half], self.device(0, 1 - 2 * half))
        elif b == 1:
            self.copies.send(self.base + 14, self.sums.at[1, self.rows(1)],
                             self.left2.at[self.rows(1)], self.device(0, 1))
        else:
            self.copies.send(self.base + 15, self.sums.at[3, self.rows(0)],
                             self.right2.at[self.rows(0)], self.device(0, -1))

    def join2(self, half):
        self.copies.arrived(self.base + 12 + half, self.passing2.at[half])
        b = 1 if half == 0 else 3
        mine = self.sums[b, self.rows(half)].astype(jnp.float32)
        self.joined2[half] = (mine + self.passing2[half].astype(jnp.float32)).astype(jnp.bfloat16)
        if half == 0:
            self.copies.send(self.base + 16, self.joined2.at[0], self.left2.at[self.rows(0)],
                             self.device(0, 1))
        else:
            self.copies.send(self.base + 17, self.joined2.at[1], self.right2.at[self.rows(1)],
                             self.device(0, -1))

    def end(self):
        self.copies.arrived(self.base + 14, self.left2.at[self.rows(1)])
        self.copies.arrived(self.base + 15, self.right2.at[self.rows(0)])
        self.copies.arrived(self.base + 16, self.left2.at[self.rows(0)])
        self.copies.arrived(self.base + 17, self.right2.at[self.rows(1)])
        total = self.own_sum[...] + self.left2[...].astype(jnp.float32) + self.right2[...].astype(jnp.float32)
        self.out[...] = total.astype(jnp.bfloat16)


def collect_kernel(dk_ref, dv_ref, dk_out, dv_out, passing, joined, left, right, sums, own_sum,
                   passing2, joined2, left2, right2, send_sems, recv_sems):
    copies = Copies(send_sems, recv_sems)
    k_sum, v_sum = [
        Collect(i == 0, blocks, out, copies, 18 * i, passing.at[i], joined.at[i], left.at[i], right.at[i],
                sums.at[i], own_sum.at[i], passing2.at[i], joined2.at[i], left2.at[i], right2.at[i])
        for i, (blocks, out) in enumerate(((dk_ref, dk_out), (dv_ref, dv_out)))]
    both = (k_sum, v_sum)
    greet([(1, 0), (3, 0), (0, 1), (0, 3)])
    for one in both:
        one.begin()
    for b in (2, 1, 0, 3):
        for one in both:
            one.join(b)
    for b in (2, 1, 3):
        for one in both:
            one.total(b)
            one.begin2(b)
    for half in (0, 1):
        for one in both:
            one.join2(half)
    for one in both:
        one.total(0)
    for one in both:
        one.end()
    copies.finish()


def collect(dk, dv):
    shards, local, width = dk.shape
    bf16 = jnp.bfloat16
    vmem = pl.BlockSpec(memory_space=pltpu.VMEM)
    full = (2, SIDE, local, width)
    return pl.pallas_call(
        collect_kernel,
        out_shape=(jax.ShapeDtypeStruct((local, width), bf16),) * 2,
        in_specs=[vmem, vmem],
        out_specs=(vmem, vmem),
        scratch_shapes=[
            pltpu.VMEM(full, bf16), pltpu.VMEM(full, bf16), pltpu.VMEM(full, bf16), pltpu.VMEM(full, bf16),
            pltpu.VMEM(full, bf16), pltpu.VMEM((2, local, width), jnp.float32),
            pltpu.VMEM((2, 2, local // 2, width), bf16), pltpu.VMEM((2, 2, local // 2, width), bf16),
            pltpu.VMEM((2, local, width), bf16), pltpu.VMEM((2, local, width), bf16),
            pltpu.SemaphoreType.DMA((36,)),
            pltpu.SemaphoreType.DMA((36,)),
        ],
        compiler_params=pltpu.CompilerParams(
            collective_id=1, has_side_effects=True, vmem_limit_bytes=24 << 20),
    )(dk, dv)


SIZES = (512, 768, 1024, 1536, 2048, 2816)
CHUNK = 256


def attention_kernel(scale, me, lengths, owners, qg_ref, k_ref, v_ref, kvt,
                     out_hbm, dq_hbm, dk_ref, dv_ref,
                     dk_acc, dv_acc, s_buf, p_buf, sl_buf, out_buf, dq_buf, sems):
    if me is None:
        me = lax.axis_index("ctx")
    _, pairs, rows, width = qg_ref.shape
    shards = 2 * pairs
    keys = k_ref.shape[0]
    ndocs = lengths.shape[0]
    shard_rows = keys // shards
    block = shard_rows // shards
    half = rows // 2
    heads = half // block
    per_scale = scale * LOG2E
    f32, bf16 = jnp.float32, jnp.bfloat16

    dk_acc[...] = jnp.zeros_like(dk_acc)
    dv_acc[...] = jnp.zeros_like(dv_acc)
    lane = lax.broadcasted_iota(jnp.int32, (1, rows), 1)
    second = lane >= half
    token = jnp.where(second, lane - half, lane) // heads
    key_index = lax.broadcasted_iota(jnp.int32, (CHUNK, rows), 0)

    def copies(n):
        return (pltpu.make_async_copy(out_buf.at[n], out_hbm.at[n], sems.at[0, n]),
                pltpu.make_async_copy(dq_buf.at[n], dq_hbm.at[n], sems.at[1, n]))

    @pl.loop(0, pairs)
    def _(n):
        firsts = []
        for m in range(2):
            slot = jnp.int32(0)
            for s in range(shards):
                slot = jnp.where(owners[2 * n + m, s] == me, s, slot)
            firsts.append((2 * n + m) * shard_rows + slot * block)
        pos = jnp.where(second, firsts[1], firsts[0]) + token
        start = jnp.zeros_like(pos)
        low = jnp.int32(0)
        end = jnp.int32(0)
        for d in range(ndocs):
            end = end + lengths[d]
            start = jnp.where(end <= pos, end, start)
            low = jnp.where(end <= firsts[0], end, low)
        base = (low // 128) * 128
        need = firsts[1] + block - base

        def work(size):
            at = pl.multiple_of(jnp.minimum(base, keys - size), 128)
            lower = start - at
            upper = pos - at
            peak = jnp.full((8, rows), NEG, f32)
            for c in range(size // CHUNK):
                here = slice(c * CHUNK, (c + 1) * CHUNK)
                raw = dot(k_ref[pl.ds(at + c * CHUNK, CHUNK), :], qg_ref[0, n], NT)
                allowed = (key_index >= lower - c * CHUNK) & (key_index <= upper - c * CHUNK)
                x = jnp.where(allowed, raw, NEG)
                s_buf[here, :] = x
                peak = jnp.maximum(peak, folded(x, jnp.max))
            peak = jnp.max(peak, axis=0, keepdims=True)
            total = jnp.zeros((8, rows), f32)
            for c in range(size // CHUNK):
                here = slice(c * CHUNK, (c + 1) * CHUNK)
                p = jnp.exp2((s_buf[here, :] - peak) * per_scale)
                p_buf[here, :] = p.astype(bf16)
                total = total + folded(p, jnp.sum)
            inverse = 1.0 / jnp.sum(total, axis=0, keepdims=True)
            span = pl.ds(at, size)
            out = dot(kvt[width:2 * width, span], p_buf[0:size, :], NN)
            out = (out * inverse).T.astype(bf16)
            out_buf[n] = out
            delta = jnp.sum((out.astype(f32) * qg_ref[1, n].astype(f32)).T, axis=0, keepdims=True)
            for c in range(size // CHUNK):
                here = slice(c * CHUNK, (c + 1) * CHUNK)
                spot = pl.ds(at + c * CHUNK, CHUNK)
                products = dot(v_ref[spot, :], qg_ref[1, n], NT)
                probs = p_buf[here, :].astype(f32) * inverse
                slopes = (probs * (products - delta)).astype(bf16)
                sl_buf[here, :] = slopes
                dk_acc[spot, :] += dot(slopes, qg_ref[0, n], NN)
                dv_acc[spot, :] += dot(probs.astype(bf16), qg_ref[1, n], NN)
            dq = dot(kvt[0:width, span], sl_buf[0:size, :], NN)
            dq_buf[n] = (dq * scale).T.astype(bf16)

        for small, size in zip((0,) + SIZES, SIZES):
            @pl.when((need > small) & (need <= size))
            def _():
                work(size)

        for copy in copies(n):
            copy.start()

    @pl.loop(0, shards)
    def _(j):
        for s in range(shards):
            rows_at = pl.ds(pl.multiple_of(j * shard_rows + s * block, block), block)
            owner = owners[j, s]
            dk_ref[owner, j] = (dk_acc[rows_at, :] * scale).astype(bf16)
            dv_ref[owner, j] = dv_acc[rows_at, :].astype(bf16)

    @pl.loop(0, pairs)
    def _(n):
        for copy in copies(n):
            copy.wait()


def attention(qg, k, v, kvt, lengths, owners, me=None, interpret=False):
    _, shards, half, width = qg.shape
    rows = 2 * half
    pairs = shards // 2
    local = k.shape[1]
    keys = shards * local
    block = local // shards
    smem = pl.BlockSpec(memory_space=pltpu.SMEM)
    vmem = pl.BlockSpec(memory_space=pltpu.VMEM)
    hbm = pl.BlockSpec(memory_space=pltpu.HBM)
    f32, bf16 = jnp.float32, jnp.bfloat16
    out, dq, dk, dv = pl.pallas_call(
        functools.partial(attention_kernel, width ** -0.5, me),
        out_shape=(
            jax.ShapeDtypeStruct((pairs, rows, width), bf16),
            jax.ShapeDtypeStruct((pairs, rows, width), bf16),
            jax.ShapeDtypeStruct((shards, shards, block, width), bf16),
            jax.ShapeDtypeStruct((shards, shards, block, width), bf16),
        ),
        in_specs=[smem, smem, vmem, vmem, vmem, vmem],
        out_specs=(hbm, hbm, vmem, vmem),
        scratch_shapes=[
            pltpu.VMEM((keys, width), f32),
            pltpu.VMEM((keys, width), f32),
            pltpu.VMEM((SIZES[-1], rows), f32),
            pltpu.VMEM((SIZES[-1], rows), bf16),
            pltpu.VMEM((SIZES[-1], rows), bf16),
            pltpu.VMEM((pairs, rows, width), bf16),
            pltpu.VMEM((pairs, rows, width), bf16),
            pltpu.SemaphoreType.DMA((2, pairs)),
        ],
        compiler_params=pltpu.CompilerParams(vmem_limit_bytes=40 << 20),
        interpret=interpret,
    )(lengths, owners, qg.reshape(2, pairs, rows, width), k.reshape(keys, width), v.reshape(keys, width), kvt)
    return out, dq, dk.reshape(shards, local, width), dv.reshape(shards, local, width)


def on_device(query, keys, values, output_gradient, doc_lengths, block_owner):
    local, heads, width = query.shape
    shards = SIDE * SIDE
    rows = local // shards * heads
    qg, k, v, kvt = exchange(block_owner, query.reshape(shards, rows, width),
                             output_gradient.reshape(shards, rows, width), keys[:, 0], values[:, 0])
    out, dq, dk, dv = attention(qg, k, v, kvt, doc_lengths, block_owner)
    dk, dv = collect(dk, dv)
    return (
        out.reshape(local, heads, width),
        dq.reshape(local, heads, width),
        dk[:, None],
        dv[:, None],
    )


def solution(mesh):
    rows = P(("dp", "ctx"), "tp", None)
    return jax.shard_map(
        on_device,
        mesh=mesh,
        in_specs=(rows, rows, rows, rows, P("dp"), P("dp", None)),
        out_specs=(rows, rows, rows, rows),
        check_vma=False,
    )
```

```python
import functools

import jax
import jax.numpy as jnp
from jax import lax
from jax.experimental import pallas as pl
from jax.experimental.pallas import tpu as pltpu
from jax.sharding import PartitionSpec as P

NEG = -1e30
LOG2E = 1.4426950408889634
NT = (((1,), (1,)), ((), ()))
NN = (((1,), (0,)), ((), ()))


def dot(a, b, dims):
    return lax.dot_general(a, b, dims, preferred_element_type=jnp.float32)


def folded(x, op):
    return op(x.reshape(x.shape[0] // 8, 8, x.shape[1]), axis=0)


SIDE = 4
MESH_AXIS = "ctx"


def coordinates():
    me = lax.axis_index(MESH_AXIS)
    return lax.div(me, SIDE), lax.rem(me, SIDE)


def device_at(dz, dy):
    z, y = coordinates()
    return lax.rem(z + dz + SIDE, SIDE) * SIDE + lax.rem(y + dy + SIDE, SIDE)


def greet(offsets):
    barrier = pltpu.get_barrier_semaphore()
    for dz, dy in offsets:
        pl.semaphore_signal(barrier, inc=1, device_id={MESH_AXIS: device_at(dz, dy)},
                            device_id_type=pl.DeviceIdType.MESH)
    pl.semaphore_wait(barrier, len(offsets))


class Copies:
    def __init__(self, send_sems, recv_sems):
        self.send_sems, self.recv_sems, self.sent = send_sems, recv_sems, []

    def make(self, n, src, dst, target):
        return pltpu.make_async_remote_copy(
            src_ref=src, dst_ref=dst, send_sem=self.send_sems.at[n], recv_sem=self.recv_sems.at[n],
            device_id={MESH_AXIS: target}, device_id_type=pl.DeviceIdType.MESH)

    def send(self, n, src, dst, target):
        copy = self.make(n, src, dst, target)
        copy.start()
        self.sent.append(copy)

    def arrived(self, n, dst):
        self.make(n, dst, dst, device_at(0, 1)).wait_recv()

    def finish(self):
        for copy in self.sent:
            copy.wait_send()


OFFSETS = [(dz, dy) for dz in (0, 1, 2, 3) for dy in (0, 1, 2, 3) if (dz, dy) != (0, 0)]


class Spread:
    def __init__(self, first_is_y, own, blocks, copies, base):
        self.first_is_y, self.own, self.blocks, self.copies, self.base = first_is_y, own, blocks, copies, base
        self.half = blocks.shape[1] // 2

    def block(self, a, b):
        return device_at(b, a) if self.first_is_y else device_at(a, b)

    def part(self, a, b, half):
        block = self.blocks.at[self.block(a, b)]
        return block if half is None else block.at[pl.ds(half * self.half, self.half)]

    def number(self, stage, a, kind):
        return self.base + (kind if stage == 1 else 4 + 4 * (a % SIDE) + kind)

    def send(self, stage, a, kind, src, part):
        step = 1 if kind in (0, 2) else -1
        target = self.block(step, 0) if stage == 1 else self.block(0, step)
        self.copies.send(self.number(stage, a, kind), src, part, target)

    def start(self):
        me = self.part(0, 0, None)
        for stage in (1, 2):
            for kind in (0, 1):
                self.send(stage, 0, kind, self.own, me)

    def got(self, stage, a, kind):
        along = {0: -1, 1: 1, 2: 2, 3: 2}[kind]
        half = {0: None, 1: None, 2: 0, 3: 1}[kind]
        part = self.part(along, 0, half) if stage == 1 else self.part(a, along, half)
        self.copies.arrived(self.number(stage, a, kind), part)

    def onward(self, stage, a, kind):
        along = -1 if kind == 0 else 1
        half = kind
        part = self.part(along, 0, half) if stage == 1 else self.part(a, along, half)
        self.send(stage, a, kind + 2, part, part)

    def second(self, a):
        part = self.part(a, 0, None)
        for kind in (0, 1):
            self.send(2, a, kind, part, part)


def exchange_kernel(owners, q_hbm, g_hbm, k_hbm, v_hbm, qg_out, k_out, v_out, kvt,
                    q_in, g_in, staging, load_sems, send_sems, recv_sems):
    me = lax.axis_index(MESH_AXIS)
    width = k_out.shape[2]
    loads = [pltpu.make_async_copy(src, dst, load_sems.at[n]) for n, (src, dst) in enumerate((
        (k_hbm, k_out.at[me]), (v_hbm, v_out.at[me]), (q_hbm, q_in), (g_hbm, g_in)))]
    for load in loads:
        load.start()
    copies = Copies(send_sems, recv_sems)
    spreads = (Spread(True, k_out.at[me], k_out, copies, 0), Spread(False, v_out.at[me], v_out, copies, 20))
    greet(OFFSETS)
    loads[0].wait()
    loads[1].wait()
    for spread in spreads:
        spread.start()
    loads[2].wait()
    loads[3].wait()

    def slot_for(target):
        slot = jnp.int32(0)
        for s in range(SIDE * SIDE):
            slot = jnp.where(owners[me, s] == target, s, slot)
        return slot

    def reassign(items):
        for n in items:
            target = device_at(*OFFSETS[n])
            slot = slot_for(target)
            staging[n, 0] = q_in[slot]
            staging[n, 1] = g_in[slot]
            copies.send(40 + n, staging.at[n], qg_out.at[:, me], target)

    far = sorted(range(15), key=lambda n: -sum(min(d, SIDE - d) for d in OFFSETS[n]))
    reassign(far[:5])
    for kind in (0, 1):
        for spread in spreads:
            spread.got(1, 0, kind)
            spread.onward(1, 0, kind)
            spread.second(-1 if kind == 0 else 1)
    reassign(far[5:10])
    for spread in spreads:
        spread.got(1, 0, 2)
        spread.got(1, 0, 3)
        spread.second(2)
    for kind in (0, 1):
        for spread in spreads:
            spread.got(2, 0, kind)
            spread.onward(2, 0, kind)
    reassign(far[10:])
    slot = slot_for(me)
    qg_out[0, me] = q_in[slot]
    qg_out[1, me] = g_in[slot]
    for a in (-1, 1, 2):
        for kind in (0, 1):
            for spread in spreads:
                spread.got(2, a, kind)
                spread.onward(2, a, kind)
    for a in (0, -1, 1, 2):
        for kind in (2, 3):
            for spread in spreads:
                spread.got(2, a, kind)

    @pl.loop(0, SIDE * SIDE)
    def _(b):
        for h in range(k_out.shape[1] // 128):
            at = pl.ds(pl.multiple_of(b * k_out.shape[1] + h * 128, 128), 128)
            kvt[0:width, at] = k_out[b, h * 128:(h + 1) * 128].T
            kvt[width:2 * width, at] = v_out[b, h * 128:(h + 1) * 128].T

    for n in far:
        dz, dy = OFFSETS[n]
        copies.arrived(40 + n, qg_out.at[:, device_at(-dz, -dy)])
    copies.finish()


def exchange(owners, q, g, k, v):
    shards, rows, width = q.shape
    local = k.shape[0]
    smem = pl.BlockSpec(memory_space=pltpu.SMEM)
    vmem = pl.BlockSpec(memory_space=pltpu.VMEM)
    hbm = pl.BlockSpec(memory_space=pltpu.HBM)
    bf16 = jnp.bfloat16
    return pl.pallas_call(
        exchange_kernel,
        out_shape=(
            jax.ShapeDtypeStruct((2, shards, rows, width), bf16),
            jax.ShapeDtypeStruct((shards, local, width), bf16),
            jax.ShapeDtypeStruct((shards, local, width), bf16),
            jax.ShapeDtypeStruct((2 * width, shards * local), bf16),
        ),
        in_specs=[smem, hbm, hbm, hbm, hbm],
        out_specs=(vmem, vmem, vmem, vmem),
        scratch_shapes=[
            pltpu.VMEM((shards, rows, width), bf16),
            pltpu.VMEM((shards, rows, width), bf16),
            pltpu.VMEM((shards - 1, 2, rows, width), bf16),
            pltpu.SemaphoreType.DMA((4,)),
            pltpu.SemaphoreType.DMA((55,)),
            pltpu.SemaphoreType.DMA((55,)),
        ],
        compiler_params=pltpu.CompilerParams(
            collective_id=0, has_side_effects=True, vmem_limit_bytes=24 << 20),
    )(owners, q, g, k, v)


class Collect:
    PLUS, MINUS = (2, 0), (1, 3)

    def __init__(self, first_is_y, blocks, out, copies, base, passing, joined, left, right,
                 sums, own_sum, passing2, joined2, left2, right2):
        self.first_is_y, self.blocks, self.out, self.copies, self.base = first_is_y, blocks, out, copies, base
        self.passing, self.joined, self.left, self.right = passing, joined, left, right
        self.sums, self.own_sum = sums, own_sum
        self.passing2, self.joined2, self.left2, self.right2 = passing2, joined2, left2, right2
        self.half = out.shape[0] // 2

    def device(self, a, b):
        return device_at(b, a) if self.first_is_y else device_at(a, b)

    def begin(self):
        for b in (2, 1, 0, 3):
            step = 1 if b in self.PLUS else -1
            self.copies.send(self.base + b, self.blocks.at[self.device(2, b)], self.passing.at[b],
                             self.device(step, 0))
        for b in (2, 1, 3, 0):
            if b in self.PLUS:
                self.copies.send(self.base + 8 + b, self.blocks.at[self.device(-1, b)],
                                 self.right.at[b], self.device(-1, 0))
            else:
                self.copies.send(self.base + 4 + b, self.blocks.at[self.device(1, b)],
                                 self.left.at[b], self.device(1, 0))

    def join(self, b):
        self.copies.arrived(self.base + b, self.passing.at[b])
        step = 1 if b in self.PLUS else -1
        mine = self.blocks[self.device(step, b)].astype(jnp.float32)
        self.joined[b] = (mine + self.passing[b].astype(jnp.float32)).astype(jnp.bfloat16)
        if step == 1:
            self.copies.send(self.base + 4 + b, self.joined.at[b], self.left.at[b], self.device(1, 0))
        else:
            self.copies.send(self.base + 8 + b, self.joined.at[b], self.right.at[b], self.device(-1, 0))

    def total(self, b):
        self.copies.arrived(self.base + 4 + b, self.left.at[b])
        self.copies.arrived(self.base + 8 + b, self.right.at[b])
        total = (self.blocks[self.device(0, b)].astype(jnp.float32)
                 + self.left[b].astype(jnp.float32) + self.right[b].astype(jnp.float32))
        if b == 0:
            self.own_sum[...] = total
        else:
            self.sums[b] = total.astype(jnp.bfloat16)

    def rows(self, half):
        return pl.ds(half * self.half, self.half)

    def begin2(self, b):
        if b == 2:
            for half in (0, 1):
                self.copies.send(self.base + 12 + half, self.sums.at[2, self.rows(half)],
                                 self.passing2.at[half], self.device(0, 1 - 2 * half))
        elif b == 1:
            self.copies.send(self.base + 14, self.sums.at[1, self.rows(1)],
                             self.left2.at[self.rows(1)], self.device(0, 1))
        else:
            self.copies.send(self.base + 15, self.sums.at[3, self.rows(0)],
                             self.right2.at[self.rows(0)], self.device(0, -1))

    def join2(self, half):
        self.copies.arrived(self.base + 12 + half, self.passing2.at[half])
        b = 1 if half == 0 else 3
        mine = self.sums[b, self.rows(half)].astype(jnp.float32)
        self.joined2[half] = (mine + self.passing2[half].astype(jnp.float32)).astype(jnp.bfloat16)
        if half == 0:
            self.copies.send(self.base + 16, self.joined2.at[0], self.left2.at[self.rows(0)],
                             self.device(0, 1))
        else:
            self.copies.send(self.base + 17, self.joined2.at[1], self.right2.at[self.rows(1)],
                             self.device(0, -1))

    def end(self):
        self.copies.arrived(self.base + 14, self.left2.at[self.rows(1)])
        self.copies.arrived(self.base + 15, self.right2.at[self.rows(0)])
        self.copies.arrived(self.base + 16, self.left2.at[self.rows(0)])
        self.copies.arrived(self.base + 17, self.right2.at[self.rows(1)])
        total = self.own_sum[...] + self.left2[...].astype(jnp.float32) + self.right2[...].astype(jnp.float32)
        self.out[...] = total.astype(jnp.bfloat16)


def collect_kernel(dk_ref, dv_ref, dk_out, dv_out, passing, joined, left, right, sums, own_sum,
                   passing2, joined2, left2, right2, send_sems, recv_sems):
    copies = Copies(send_sems, recv_sems)
    k_sum, v_sum = [
        Collect(i == 0, blocks, out, copies, 18 * i, passing.at[i], joined.at[i], left.at[i], right.at[i],
                sums.at[i], own_sum.at[i], passing2.at[i], joined2.at[i], left2.at[i], right2.at[i])
        for i, (blocks, out) in enumerate(((dk_ref, dk_out), (dv_ref, dv_out)))]
    both = (k_sum, v_sum)
    greet([(1, 0), (3, 0), (0, 1), (0, 3)])
    for one in both:
        one.begin()
    for b in (2, 1, 0, 3):
        for one in both:
            one.join(b)
    for b in (2, 1, 3):
        for one in both:
            one.total(b)
            one.begin2(b)
    for half in (0, 1):
        for one in both:
            one.join2(half)
    for one in both:
        one.total(0)
    for one in both:
        one.end()
    copies.finish()


def collect(dk, dv):
    shards, local, width = dk.shape
    bf16 = jnp.bfloat16
    vmem = pl.BlockSpec(memory_space=pltpu.VMEM)
    full = (2, SIDE, local, width)
    return pl.pallas_call(
        collect_kernel,
        out_shape=(jax.ShapeDtypeStruct((local, width), bf16),) * 2,
        in_specs=[vmem, vmem],
        out_specs=(vmem, vmem),
        scratch_shapes=[
            pltpu.VMEM(full, bf16), pltpu.VMEM(full, bf16), pltpu.VMEM(full, bf16), pltpu.VMEM(full, bf16),
            pltpu.VMEM(full, bf16), pltpu.VMEM((2, local, width), jnp.float32),
            pltpu.VMEM((2, 2, local // 2, width), bf16), pltpu.VMEM((2, 2, local // 2, width), bf16),
            pltpu.VMEM((2, local, width), bf16), pltpu.VMEM((2, local, width), bf16),
            pltpu.SemaphoreType.DMA((36,)),
            pltpu.SemaphoreType.DMA((36,)),
        ],
        compiler_params=pltpu.CompilerParams(
            collective_id=1, has_side_effects=True, vmem_limit_bytes=24 << 20),
    )(dk, dv)


SIZES = (256, 512, 768, 1024, 1536, 2304)
CHUNK = 256


def attention_kernel(scale, me, lengths, owners, qg_ref, k_ref, v_ref, kvt,
                     out_hbm, dq_hbm, dk_ref, dv_ref,
                     dk_acc, dv_acc, out_buf, dq_buf, sems, *lanes):
    if me is None:
        me = lax.axis_index("ctx")
    _, shards, rows, width = qg_ref.shape
    keys = k_ref.shape[0]
    ndocs = lengths.shape[0]
    shard_rows = keys // shards
    block = shard_rows // shards
    heads = rows // block
    per_scale = scale * LOG2E
    f32, bf16 = jnp.float32, jnp.bfloat16
    together = len(lanes) // 3
    lanes = [lanes[3 * n:3 * n + 3] for n in range(together)]

    dk_acc[...] = jnp.zeros_like(dk_acc)
    dv_acc[...] = jnp.zeros_like(dv_acc)
    token = lax.broadcasted_iota(jnp.int32, (1, rows), 1) // heads
    key_index = lax.broadcasted_iota(jnp.int32, (CHUNK, rows), 0)

    def copies(j):
        return (pltpu.make_async_copy(out_buf.at[j], out_hbm.at[j], sems.at[0, j]),
                pltpu.make_async_copy(dq_buf.at[j], dq_hbm.at[j], sems.at[1, j]))

    class Segment:
        def __init__(self, j, lane):
            self.j = j
            self.q, self.g = qg_ref.at[0, j], qg_ref.at[1, j]
            self.s_buf, self.d_buf, self.sp_buf = lanes[lane]
            slot = jnp.int32(0)
            for s in range(shards):
                slot = jnp.where(owners[j, s] == me, s, slot)
            first = j * shard_rows + slot * block
            self.pos = first + token
            start = jnp.zeros_like(self.pos)
            low = jnp.int32(0)
            end = jnp.int32(0)
            for d in range(ndocs):
                end = end + lengths[d]
                start = jnp.where(end <= self.pos, end, start)
                low = jnp.where(end <= first, end, low)
            self.start = start
            self.base = (low // 128) * 128
            self.need = first + block - self.base

        def open(self, size):
            self.size = size
            self.at = pl.multiple_of(jnp.minimum(self.base, keys - size), 128)
            self.lower = self.start - self.at
            self.upper = self.pos - self.at
            self.peak = jnp.full((8, rows), NEG, f32)
            self.total = jnp.zeros((8, rows), f32)
            self.dsum = jnp.zeros((8, rows), f32)

        def scores(self, c):
            here = slice(c * CHUNK, (c + 1) * CHUNK)
            span = pl.ds(self.at + c * CHUNK, CHUNK)
            raw = dot(k_ref[span, :], self.q[...], NT)
            self.d_buf[here, :] = dot(v_ref[span, :], self.g[...], NT)
            allowed = (key_index >= self.lower - c * CHUNK) & (key_index <= self.upper - c * CHUNK)
            x = jnp.where(allowed, raw, NEG)
            self.s_buf[here, :] = x
            self.peak = jnp.maximum(self.peak, folded(x, jnp.max))

        def peaked(self):
            self.peak = jnp.max(self.peak, axis=0, keepdims=True)

        def weights(self, c):
            here = slice(c * CHUNK, (c + 1) * CHUNK)
            p = jnp.exp2((self.s_buf[here, :] - self.peak) * per_scale)
            self.s_buf[here, :] = p
            self.total = self.total + folded(p, jnp.sum)
            self.dsum = self.dsum + folded(p * self.d_buf[here, :], jnp.sum)

        def summed(self):
            self.inverse = 1.0 / jnp.sum(self.total, axis=0, keepdims=True)
            self.delta = jnp.sum(self.dsum, axis=0, keepdims=True) * self.inverse

        def slopes(self, c):
            here = slice(c * CHUNK, (c + 1) * CHUNK)
            probs = self.s_buf[here, :] * self.inverse
            slopes = probs * (self.d_buf[here, :] - self.delta)
            slopes, probs = slopes.astype(bf16), probs.astype(bf16)
            self.sp_buf[here, 0:rows] = slopes
            self.sp_buf[here, rows:2 * rows] = probs
            spot = pl.ds(self.at + c * CHUNK, CHUNK)
            dk_acc[spot, :] += dot(slopes, self.q[...], NN)
            dv_acc[spot, :] += dot(probs, self.g[...], NN)

        def finish(self):
            span = pl.ds(self.at, self.size)
            here = slice(0, self.size)
            dq = dot(kvt[0:width, span], self.sp_buf[here, 0:rows], NN)
            out = dot(kvt[width:2 * width, span], self.sp_buf[here, rows:2 * rows], NN)
            dq_buf[self.j] = (dq * scale).T.astype(bf16)
            out_buf[self.j] = out.T.astype(bf16)

    def work(segments, size):
        chunks = range(size // CHUNK)
        for one in segments:
            one.open(size)
        for c in chunks:
            segments[0].scores(c)
        segments[0].peaked()
        if len(segments) == 1:
            for c in chunks:
                segments[0].weights(c)
            segments[0].summed()
            for c in chunks:
                segments[0].slopes(c)
            segments[0].finish()
            return
        for c in chunks:
            segments[0].weights(c)
            segments[1].scores(c)
        segments[0].summed()
        segments[1].peaked()
        for c in chunks:
            segments[0].slopes(c)
            segments[1].weights(c)
        segments[1].summed()
        segments[0].finish()
        for c in chunks:
            segments[1].slopes(c)
        segments[1].finish()

    @pl.loop(0, shards // together)
    def _(n):
        segments = [Segment(n * together + m, m) for m in range(together)]
        need = segments[0].need
        for one in segments[1:]:
            need = jnp.maximum(need, one.need)
        for small, size in zip((0,) + SIZES, SIZES):
            @pl.when((need > small) & (need <= size))
            def _():
                work(segments, size)

        for one in segments:
            for copy in copies(one.j):
                copy.start()

    @pl.loop(0, shards)
    def _(j):
        for s in range(shards):
            rows_at = pl.ds(pl.multiple_of(j * shard_rows + s * block, block), block)
            owner = owners[j, s]
            dk_ref[owner, j] = (dk_acc[rows_at, :] * scale).astype(bf16)
            dv_ref[owner, j] = dv_acc[rows_at, :].astype(bf16)

    @pl.loop(0, shards)
    def _(j):
        for copy in copies(j):
            copy.wait()


def attention(qg, k, v, kvt, lengths, owners, me=None, interpret=False):
    _, shards, rows, width = qg.shape
    local = k.shape[1]
    keys = shards * local
    block = keys // shards // shards
    smem = pl.BlockSpec(memory_space=pltpu.SMEM)
    vmem = pl.BlockSpec(memory_space=pltpu.VMEM)
    hbm = pl.BlockSpec(memory_space=pltpu.HBM)
    f32, bf16 = jnp.float32, jnp.bfloat16
    out, dq, dk, dv = pl.pallas_call(
        functools.partial(attention_kernel, width ** -0.5, me),
        out_shape=(
            jax.ShapeDtypeStruct((shards, rows, width), bf16),
            jax.ShapeDtypeStruct((shards, rows, width), bf16),
            jax.ShapeDtypeStruct((shards, shards, block, width), bf16),
            jax.ShapeDtypeStruct((shards, shards, block, width), bf16),
        ),
        in_specs=[smem, smem, vmem, vmem, vmem, vmem],
        out_specs=(hbm, hbm, vmem, vmem),
        scratch_shapes=[
            pltpu.VMEM((keys, width), f32),
            pltpu.VMEM((keys, width), f32),
            pltpu.VMEM((shards, rows, width), bf16),
            pltpu.VMEM((shards, rows, width), bf16),
            pltpu.SemaphoreType.DMA((2, shards)),
        ] + 2 * [
            pltpu.VMEM((SIZES[-1], rows), f32),
            pltpu.VMEM((SIZES[-1], rows), f32),
            pltpu.VMEM((SIZES[-1], 2 * rows), bf16),
        ],
        compiler_params=pltpu.CompilerParams(vmem_limit_bytes=40 << 20),
        interpret=interpret,
    )(lengths, owners, qg, k.reshape(keys, width), v.reshape(keys, width), kvt)
    return out, dq, dk.reshape(shards, local, width), dv.reshape(shards, local, width)


def on_device(query, keys, values, output_gradient, doc_lengths, block_owner):
    local, heads, width = query.shape
    shards = SIDE * SIDE
    rows = local // shards * heads
    qg, k, v, kvt = exchange(block_owner, query.reshape(shards, rows, width),
                             output_gradient.reshape(shards, rows, width), keys[:, 0], values[:, 0])
    out, dq, dk, dv = attention(qg, k, v, kvt, doc_lengths, block_owner)
    dk, dv = collect(dk, dv)
    return (
        out.reshape(local, heads, width),
        dq.reshape(local, heads, width),
        dk[:, None],
        dv[:, None],
    )


def solution(mesh):
    rows = P(("dp", "ctx"), "tp", None)
    return jax.shard_map(
        on_device,
        mesh=mesh,
        in_specs=(rows, rows, rows, rows, P("dp"), P("dp", None)),
        out_specs=(rows, rows, rows, rows),
        check_vma=False,
    )
```

```python
import functools

import jax
import jax.numpy as jnp
from jax import lax
from jax.experimental import pallas as pl
from jax.experimental.pallas import tpu as pltpu
from jax.sharding import PartitionSpec as P

NEG = -1e30
LOG2E = 1.4426950408889634
NT = (((1,), (1,)), ((), ()))
NN = (((1,), (0,)), ((), ()))


def dot(a, b, dims):
    return lax.dot_general(a, b, dims, preferred_element_type=jnp.float32)


def folded(x, op):
    return op(x.reshape(x.shape[0] // 8, 8, x.shape[1]), axis=0)


SIDE = 4
MESH_AXIS = "ctx"


def coordinates():
    me = lax.axis_index(MESH_AXIS)
    return lax.div(me, SIDE), lax.rem(me, SIDE)


def device_at(dz, dy):
    z, y = coordinates()
    return lax.rem(z + dz + SIDE, SIDE) * SIDE + lax.rem(y + dy + SIDE, SIDE)


def greet(offsets):
    barrier = pltpu.get_barrier_semaphore()
    for dz, dy in offsets:
        pl.semaphore_signal(barrier, inc=1, device_id={MESH_AXIS: device_at(dz, dy)},
                            device_id_type=pl.DeviceIdType.MESH)
    pl.semaphore_wait(barrier, len(offsets))


class Copies:
    def __init__(self, send_sems, recv_sems):
        self.send_sems, self.recv_sems, self.sent = send_sems, recv_sems, []

    def make(self, n, src, dst, target):
        return pltpu.make_async_remote_copy(
            src_ref=src, dst_ref=dst, send_sem=self.send_sems.at[n], recv_sem=self.recv_sems.at[n],
            device_id={MESH_AXIS: target}, device_id_type=pl.DeviceIdType.MESH)

    def send(self, n, src, dst, target):
        copy = self.make(n, src, dst, target)
        copy.start()
        self.sent.append(copy)

    def arrived(self, n, dst):
        self.make(n, dst, dst, device_at(0, 1)).wait_recv()

    def finish(self):
        for copy in self.sent:
            copy.wait_send()


OFFSETS = [(dz, dy) for dz in (0, 1, 2, 3) for dy in (0, 1, 2, 3) if (dz, dy) != (0, 0)]


class Spread:
    def __init__(self, first_is_y, own, blocks, copies, base):
        self.first_is_y, self.own, self.blocks, self.copies, self.base = first_is_y, own, blocks, copies, base
        self.half = blocks.shape[1] // 2

    def block(self, a, b):
        return device_at(b, a) if self.first_is_y else device_at(a, b)

    def part(self, a, b, half):
        block = self.blocks.at[self.block(a, b)]
        return block if half is None else block.at[pl.ds(half * self.half, self.half)]

    def number(self, stage, a, kind):
        return self.base + (kind if stage == 1 else 4 + 4 * (a % SIDE) + kind)

    def send(self, stage, a, kind, src, part):
        step = 1 if kind in (0, 2) else -1
        target = self.block(step, 0) if stage == 1 else self.block(0, step)
        self.copies.send(self.number(stage, a, kind), src, part, target)

    def start(self):
        me = self.part(0, 0, None)
        for stage in (1, 2):
            for kind in (0, 1):
                self.send(stage, 0, kind, self.own, me)

    def got(self, stage, a, kind):
        along = {0: -1, 1: 1, 2: 2, 3: 2}[kind]
        half = {0: None, 1: None, 2: 0, 3: 1}[kind]
        part = self.part(along, 0, half) if stage == 1 else self.part(a, along, half)
        self.copies.arrived(self.number(stage, a, kind), part)

    def onward(self, stage, a, kind):
        along = -1 if kind == 0 else 1
        half = kind
        part = self.part(along, 0, half) if stage == 1 else self.part(a, along, half)
        self.send(stage, a, kind + 2, part, part)

    def second(self, a):
        part = self.part(a, 0, None)
        for kind in (0, 1):
            self.send(2, a, kind, part, part)


def exchange_kernel(owners, q_hbm, g_hbm, k_hbm, v_hbm, qg_out, k_out, v_out, kvt,
                    q_in, g_in, staging, load_sems, send_sems, recv_sems):
    me = lax.axis_index(MESH_AXIS)
    width = k_out.shape[2]
    loads = [pltpu.make_async_copy(src, dst, load_sems.at[n]) for n, (src, dst) in enumerate((
        (k_hbm, k_out.at[me]), (v_hbm, v_out.at[me]), (q_hbm, q_in), (g_hbm, g_in)))]
    for load in loads:
        load.start()
    copies = Copies(send_sems, recv_sems)
    spreads = (Spread(True, k_out.at[me], k_out, copies, 0), Spread(False, v_out.at[me], v_out, copies, 20))
    greet(OFFSETS)
    loads[0].wait()
    loads[1].wait()
    for spread in spreads:
        spread.start()
    loads[2].wait()
    loads[3].wait()

    def turn(spread, a, b):
        row = 0 if spread.first_is_y else width
        block = spread.block(a, b)
        for h in range(k_out.shape[1] // 128):
            at = pl.ds(pl.multiple_of(block * k_out.shape[1] + h * 128, 128), 128)
            kvt[row:row + width, at] = spread.blocks[block, h * 128:(h + 1) * 128].T

    def slot_for(target):
        slot = jnp.int32(0)
        for s in range(SIDE * SIDE):
            slot = jnp.where(owners[me, s] == target, s, slot)
        return slot

    def reassign(items):
        for n in items:
            target = device_at(*OFFSETS[n])
            slot = slot_for(target)
            staging[n, 0] = q_in[slot]
            staging[n, 1] = g_in[slot]
            copies.send(40 + n, staging.at[n], qg_out.at[:, me], target)

    far = sorted(range(15), key=lambda n: -sum(min(d, SIDE - d) for d in OFFSETS[n]))
    reassign(far[:5])
    for kind in (0, 1):
        for spread in spreads:
            spread.got(1, 0, kind)
            spread.onward(1, 0, kind)
            spread.second(-1 if kind == 0 else 1)
    for spread in spreads:
        for a in (0, -1, 1):
            turn(spread, a, 0)
    reassign(far[5:10])
    for spread in spreads:
        spread.got(1, 0, 2)
        spread.got(1, 0, 3)
        spread.second(2)
    for spread in spreads:
        turn(spread, 2, 0)
    for kind in (0, 1):
        for spread in spreads:
            spread.got(2, 0, kind)
            spread.onward(2, 0, kind)
    reassign(far[10:])
    slot = slot_for(me)
    qg_out[0, me] = q_in[slot]
    qg_out[1, me] = g_in[slot]
    for a in (-1, 1, 2):
        for kind in (0, 1):
            for spread in spreads:
                spread.got(2, a, kind)
                spread.onward(2, a, kind)
    for spread in spreads:
        for a in (0, -1, 1, 2):
            for b in (-1, 1):
                turn(spread, a, b)
    for a in (0, -1, 1, 2):
        for kind in (2, 3):
            for spread in spreads:
                spread.got(2, a, kind)
        for spread in spreads:
            turn(spread, a, 2)

    for n in far:
        dz, dy = OFFSETS[n]
        copies.arrived(40 + n, qg_out.at[:, device_at(-dz, -dy)])
    copies.finish()


def exchange(owners, q, g, k, v):
    shards, rows, width = q.shape
    local = k.shape[0]
    smem = pl.BlockSpec(memory_space=pltpu.SMEM)
    vmem = pl.BlockSpec(memory_space=pltpu.VMEM)
    hbm = pl.BlockSpec(memory_space=pltpu.HBM)
    bf16 = jnp.bfloat16
    return pl.pallas_call(
        exchange_kernel,
        out_shape=(
            jax.ShapeDtypeStruct((2, shards, rows, width), bf16),
            jax.ShapeDtypeStruct((shards, local, width), bf16),
            jax.ShapeDtypeStruct((shards, local, width), bf16),
            jax.ShapeDtypeStruct((2 * width, shards * local), bf16),
        ),
        in_specs=[smem, hbm, hbm, hbm, hbm],
        out_specs=(vmem, vmem, vmem, vmem),
        scratch_shapes=[
            pltpu.VMEM((shards, rows, width), bf16),
            pltpu.VMEM((shards, rows, width), bf16),
            pltpu.VMEM((shards - 1, 2, rows, width), bf16),
            pltpu.SemaphoreType.DMA((4,)),
            pltpu.SemaphoreType.DMA((55,)),
            pltpu.SemaphoreType.DMA((55,)),
        ],
        compiler_params=pltpu.CompilerParams(
            collective_id=0, has_side_effects=True, vmem_limit_bytes=24 << 20),
    )(owners, q, g, k, v)


class Collect:
    PLUS, MINUS = (2, 0), (1, 3)

    def __init__(self, first_is_y, blocks, out, copies, base, passing, joined, left, right,
                 sums, own_sum, far2, left2, right2):
        self.first_is_y, self.blocks, self.out, self.copies, self.base = first_is_y, blocks, out, copies, base
        self.passing, self.joined, self.left, self.right = passing, joined, left, right
        self.sums, self.own_sum = sums, own_sum
        self.far2, self.left2, self.right2 = far2, left2, right2

    def device(self, a, b):
        return device_at(b, a) if self.first_is_y else device_at(a, b)

    def begin(self):
        for b in (2, 1, 0, 3):
            step = 1 if b in self.PLUS else -1
            self.copies.send(self.base + b, self.blocks.at[self.device(2, b)], self.passing.at[b],
                             self.device(step, 0))
        for b in (2, 1, 3, 0):
            if b in self.PLUS:
                self.copies.send(self.base + 8 + b, self.blocks.at[self.device(-1, b)],
                                 self.right.at[b], self.device(-1, 0))
            else:
                self.copies.send(self.base + 4 + b, self.blocks.at[self.device(1, b)],
                                 self.left.at[b], self.device(1, 0))

    def join(self, b):
        self.copies.arrived(self.base + b, self.passing.at[b])
        step = 1 if b in self.PLUS else -1
        mine = self.blocks[self.device(step, b)].astype(jnp.float32)
        self.joined[b] = (mine + self.passing[b].astype(jnp.float32)).astype(jnp.bfloat16)
        if step == 1:
            self.copies.send(self.base + 4 + b, self.joined.at[b], self.left.at[b], self.device(1, 0))
        else:
            self.copies.send(self.base + 8 + b, self.joined.at[b], self.right.at[b], self.device(-1, 0))

    def total(self, b):
        self.copies.arrived(self.base + 4 + b, self.left.at[b])
        self.copies.arrived(self.base + 8 + b, self.right.at[b])
        total = (self.blocks[self.device(0, b)].astype(jnp.float32)
                 + self.left[b].astype(jnp.float32) + self.right[b].astype(jnp.float32))
        if b == 0:
            self.own_sum[...] = total
        else:
            self.sums[b] = total.astype(jnp.bfloat16)

    def begin2(self, b):
        land = {1: self.left2, 2: self.far2, 3: self.right2}[b]
        self.copies.send(self.base + 11 + b, self.sums.at[b], land, self.device(0, b))

    def end(self):
        total = self.own_sum[...]
        for b, land in ((1, self.left2), (2, self.far2), (3, self.right2)):
            self.copies.arrived(self.base + 11 + b, land)
            total = total + land[...].astype(jnp.float32)
        self.out[...] = total.astype(jnp.bfloat16)


def collect_kernel(dk_ref, dv_ref, dk_out, dv_out, passing, joined, left, right, sums, own_sum,
                   far2, left2, right2, send_sems, recv_sems):
    copies = Copies(send_sems, recv_sems)
    k_sum, v_sum = [
        Collect(i == 0, blocks, out, copies, 15 * i, passing.at[i], joined.at[i], left.at[i], right.at[i],
                sums.at[i], own_sum.at[i], far2.at[i], left2.at[i], right2.at[i])
        for i, (blocks, out) in enumerate(((dk_ref, dk_out), (dv_ref, dv_out)))]
    both = (k_sum, v_sum)
    greet([(1, 0), (2, 0), (3, 0), (0, 1), (0, 2), (0, 3)])
    for one in both:
        one.begin()
    for b in (2, 1, 0, 3):
        for one in both:
            one.join(b)
    for b in (2, 1, 3):
        for one in both:
            one.total(b)
            one.begin2(b)
    for one in both:
        one.total(0)
    for one in both:
        one.end()
    copies.finish()


def collect(dk, dv):
    shards, local, width = dk.shape
    bf16 = jnp.bfloat16
    vmem = pl.BlockSpec(memory_space=pltpu.VMEM)
    full = (2, SIDE, local, width)
    return pl.pallas_call(
        collect_kernel,
        out_shape=(jax.ShapeDtypeStruct((local, width), bf16),) * 2,
        in_specs=[vmem, vmem],
        out_specs=(vmem, vmem),
        scratch_shapes=[
            pltpu.VMEM(full, bf16), pltpu.VMEM(full, bf16), pltpu.VMEM(full, bf16), pltpu.VMEM(full, bf16),
            pltpu.VMEM(full, bf16), pltpu.VMEM((2, local, width), jnp.float32),
            pltpu.VMEM((2, local, width), bf16), pltpu.VMEM((2, local, width), bf16), pltpu.VMEM((2, local, width), bf16),
            pltpu.SemaphoreType.DMA((30,)),
            pltpu.SemaphoreType.DMA((30,)),
        ],
        compiler_params=pltpu.CompilerParams(
            collective_id=1, has_side_effects=True, vmem_limit_bytes=24 << 20),
    )(dk, dv)


SIZES = (256, 512, 768, 1024, 1536, 2304)
CHUNK = 256


def attention_kernel(scale, me, lengths, owners, qg_ref, k_ref, v_ref, kvt,
                     out_hbm, dq_hbm, dk_ref, dv_ref,
                     dk_acc, dv_acc, out_buf, dq_buf, sems, *lanes):
    if me is None:
        me = lax.axis_index("ctx")
    _, shards, rows, width = qg_ref.shape
    keys = k_ref.shape[0]
    ndocs = lengths.shape[0]
    shard_rows = keys // shards
    block = shard_rows // shards
    heads = rows // block
    per_scale = scale * LOG2E
    f32, bf16 = jnp.float32, jnp.bfloat16
    together = len(lanes) // 3
    lanes = [lanes[3 * n:3 * n + 3] for n in range(together)]

    dk_acc[...] = jnp.zeros_like(dk_acc)
    dv_acc[...] = jnp.zeros_like(dv_acc)
    token = lax.broadcasted_iota(jnp.int32, (1, rows), 1) // heads
    key_index = lax.broadcasted_iota(jnp.int32, (CHUNK, rows), 0)

    def copies(j):
        return (pltpu.make_async_copy(out_buf.at[j], out_hbm.at[j], sems.at[0, j]),
                pltpu.make_async_copy(dq_buf.at[j], dq_hbm.at[j], sems.at[1, j]))

    class Segment:
        def __init__(self, j, lane):
            self.j = j
            self.q, self.g = qg_ref.at[0, j], qg_ref.at[1, j]
            self.s_buf, self.d_buf, self.sp_buf = lanes[lane]
            slot = jnp.int32(0)
            for s in range(shards):
                slot = jnp.where(owners[j, s] == me, s, slot)
            first = j * shard_rows + slot * block
            self.pos = first + token
            start = jnp.zeros_like(self.pos)
            low = jnp.int32(0)
            end = jnp.int32(0)
            for d in range(ndocs):
                end = end + lengths[d]
                start = jnp.where(end <= self.pos, end, start)
                low = jnp.where(end <= first, end, low)
            self.start = start
            self.base = (low // 128) * 128
            self.need = first + block - self.base

        def open(self, size):
            self.size = size
            self.at = pl.multiple_of(jnp.minimum(self.base, keys - size), 128)
            self.lower = self.start - self.at
            self.upper = self.pos - self.at
            self.peak = jnp.full((8, rows), NEG, f32)
            self.total = jnp.zeros((8, rows), f32)
            self.dsum = jnp.zeros((8, rows), f32)

        def scores(self, c):
            here = slice(c * CHUNK, (c + 1) * CHUNK)
            span = pl.ds(self.at + c * CHUNK, CHUNK)
            raw = dot(k_ref[span, :], self.q[...], NT)
            self.d_buf[here, :] = dot(v_ref[span, :], self.g[...], NT)
            allowed = (key_index >= self.lower - c * CHUNK) & (key_index <= self.upper - c * CHUNK)
            x = jnp.where(allowed, raw, NEG)
            self.s_buf[here, :] = x
            self.peak = jnp.maximum(self.peak, folded(x, jnp.max))

        def peaked(self):
            self.peak = jnp.max(self.peak, axis=0, keepdims=True)

        def weights(self, c):
            here = slice(c * CHUNK, (c + 1) * CHUNK)
            p = jnp.exp2((self.s_buf[here, :] - self.peak) * per_scale)
            self.s_buf[here, :] = p
            self.total = self.total + folded(p, jnp.sum)
            self.dsum = self.dsum + folded(p * self.d_buf[here, :], jnp.sum)

        def summed(self):
            self.inverse = 1.0 / jnp.sum(self.total, axis=0, keepdims=True)
            self.delta = jnp.sum(self.dsum, axis=0, keepdims=True) * self.inverse

        def slopes(self, c):
            here = slice(c * CHUNK, (c + 1) * CHUNK)
            probs = self.s_buf[here, :] * self.inverse
            slopes = probs * (self.d_buf[here, :] - self.delta)
            slopes, probs = slopes.astype(bf16), probs.astype(bf16)
            self.sp_buf[here, 0:rows] = slopes
            self.sp_buf[here, rows:2 * rows] = probs
            spot = pl.ds(self.at + c * CHUNK, CHUNK)
            dk_acc[spot, :] += dot(slopes, self.q[...], NN)
            dv_acc[spot, :] += dot(probs, self.g[...], NN)

        def finish(self):
            span = pl.ds(self.at, self.size)
            here = slice(0, self.size)
            dq = dot(kvt[0:width, span], self.sp_buf[here, 0:rows], NN)
            out = dot(kvt[width:2 * width, span], self.sp_buf[here, rows:2 * rows], NN)
            dq_buf[self.j] = (dq * scale).T.astype(bf16)
            out_buf[self.j] = out.T.astype(bf16)

    def work(segments, size):
        chunks = range(size // CHUNK)
        for one in segments:
            one.open(size)
        for c in chunks:
            segments[0].scores(c)
        segments[0].peaked()
        if len(segments) == 1:
            for c in chunks:
                segments[0].weights(c)
            segments[0].summed()
            for c in chunks:
                segments[0].slopes(c)
            segments[0].finish()
            return
        for c in chunks:
            segments[0].weights(c)
            segments[1].scores(c)
        segments[0].summed()
        segments[1].peaked()
        for c in chunks:
            segments[0].slopes(c)
            segments[1].weights(c)
        segments[1].summed()
        segments[0].finish()
        for c in chunks:
            segments[1].slopes(c)
        segments[1].finish()

    @pl.loop(0, shards // together)
    def _(n):
        segments = [Segment(n * together + m, m) for m in range(together)]
        need = segments[0].need
        for one in segments[1:]:
            need = jnp.maximum(need, one.need)
        for small, size in zip((0,) + SIZES, SIZES):
            @pl.when((need > small) & (need <= size))
            def _():
                work(segments, size)

        for one in segments:
            for copy in copies(one.j):
                copy.start()

    @pl.loop(0, shards)
    def _(j):
        for s in range(shards):
            rows_at = pl.ds(pl.multiple_of(j * shard_rows + s * block, block), block)
            owner = owners[j, s]
            dk_ref[owner, j] = (dk_acc[rows_at, :] * scale).astype(bf16)
            dv_ref[owner, j] = dv_acc[rows_at, :].astype(bf16)

    @pl.loop(0, shards)
    def _(j):
        for copy in copies(j):
            copy.wait()


def attention(qg, k, v, kvt, lengths, owners, me=None, interpret=False):
    _, shards, rows, width = qg.shape
    local = k.shape[1]
    keys = shards * local
    block = keys // shards // shards
    smem = pl.BlockSpec(memory_space=pltpu.SMEM)
    vmem = pl.BlockSpec(memory_space=pltpu.VMEM)
    hbm = pl.BlockSpec(memory_space=pltpu.HBM)
    f32, bf16 = jnp.float32, jnp.bfloat16
    out, dq, dk, dv = pl.pallas_call(
        functools.partial(attention_kernel, width ** -0.5, me),
        out_shape=(
            jax.ShapeDtypeStruct((shards, rows, width), bf16),
            jax.ShapeDtypeStruct((shards, rows, width), bf16),
            jax.ShapeDtypeStruct((shards, shards, block, width), bf16),
            jax.ShapeDtypeStruct((shards, shards, block, width), bf16),
        ),
        in_specs=[smem, smem, vmem, vmem, vmem, vmem],
        out_specs=(hbm, hbm, vmem, vmem),
        scratch_shapes=[
            pltpu.VMEM((keys, width), f32),
            pltpu.VMEM((keys, width), f32),
            pltpu.VMEM((shards, rows, width), bf16),
            pltpu.VMEM((shards, rows, width), bf16),
            pltpu.SemaphoreType.DMA((2, shards)),
        ] + 2 * [
            pltpu.VMEM((SIZES[-1], rows), f32),
            pltpu.VMEM((SIZES[-1], rows), f32),
            pltpu.VMEM((SIZES[-1], 2 * rows), bf16),
        ],
        compiler_params=pltpu.CompilerParams(vmem_limit_bytes=40 << 20),
        interpret=interpret,
    )(lengths, owners, qg, k.reshape(keys, width), v.reshape(keys, width), kvt)
    return out, dq, dk.reshape(shards, local, width), dv.reshape(shards, local, width)


def on_device(query, keys, values, output_gradient, doc_lengths, block_owner):
    local, heads, width = query.shape
    shards = SIDE * SIDE
    rows = local // shards * heads
    loaded = (query.reshape(shards, rows, width), output_gradient.reshape(shards, rows, width),
              keys[:, 0], values[:, 0])
    loaded = [pltpu.with_memory_space_constraint(one, pltpu.HBM) for one in loaded]
    qg, k, v, kvt = exchange(block_owner, *loaded)
    out, dq, dk, dv = attention(qg, k, v, kvt, doc_lengths, block_owner)
    dk, dv = collect(dk, dv)
    return (
        out.reshape(local, heads, width),
        dq.reshape(local, heads, width),
        dk[:, None],
        dv[:, None],
    )


def solution(mesh):
    rows = P(("dp", "ctx"), "tp", None)
    return jax.shard_map(
        on_device,
        mesh=mesh,
        in_specs=(rows, rows, rows, rows, P("dp"), P("dp", None)),
        out_specs=(rows, rows, rows, rows),
        check_vma=False,
    )
```

```python
import functools

import jax
import jax.numpy as jnp
from jax import lax
from jax.experimental import pallas as pl
from jax.experimental.pallas import tpu as pltpu
from jax.sharding import PartitionSpec as P

NEG = -1e30
LOG2E = 1.4426950408889634
NT = (((1,), (1,)), ((), ()))
NN = (((1,), (0,)), ((), ()))


def dot(a, b, dims):
    return lax.dot_general(a, b, dims, preferred_element_type=jnp.float32)


def folded(x, op):
    return op(x.reshape(x.shape[0] // 8, 8, x.shape[1]), axis=0)


SIDE = 4
MESH_AXIS = "ctx"


def coordinates():
    me = lax.axis_index(MESH_AXIS)
    return lax.div(me, SIDE), lax.rem(me, SIDE)


def device_at(dz, dy):
    z, y = coordinates()
    return lax.rem(z + dz + SIDE, SIDE) * SIDE + lax.rem(y + dy + SIDE, SIDE)


def greet(offsets):
    barrier = pltpu.get_barrier_semaphore()
    for dz, dy in offsets:
        pl.semaphore_signal(barrier, inc=1, device_id={MESH_AXIS: device_at(dz, dy)},
                            device_id_type=pl.DeviceIdType.MESH)
    pl.semaphore_wait(barrier, len(offsets))


class Copies:
    def __init__(self, send_sems, recv_sems):
        self.send_sems, self.recv_sems, self.sent = send_sems, recv_sems, []

    def make(self, n, src, dst, target):
        return pltpu.make_async_remote_copy(
            src_ref=src, dst_ref=dst, send_sem=self.send_sems.at[n], recv_sem=self.recv_sems.at[n],
            device_id={MESH_AXIS: target}, device_id_type=pl.DeviceIdType.MESH)

    def send(self, n, src, dst, target):
        copy = self.make(n, src, dst, target)
        copy.start()
        self.sent.append(copy)

    def arrived(self, n, dst):
        self.make(n, dst, dst, device_at(0, 1)).wait_recv()

    def finish(self):
        for copy in self.sent:
            copy.wait_send()


OFFSETS = [(dz, dy) for dz in (0, 1, 2, 3) for dy in (0, 1, 2, 3) if (dz, dy) != (0, 0)]


class Spread:
    def __init__(self, first_is_y, own, blocks, copies, base):
        self.first_is_y, self.own, self.blocks, self.copies, self.base = first_is_y, own, blocks, copies, base
        self.half = blocks.shape[1] // 2

    def block(self, a, b):
        return device_at(b, a) if self.first_is_y else device_at(a, b)

    def part(self, a, b, half):
        block = self.blocks.at[self.block(a, b)]
        return block if half is None else block.at[pl.ds(half * self.half, self.half)]

    def number(self, stage, a, kind):
        return self.base + (kind if stage == 1 else 4 + 4 * (a % SIDE) + kind)

    def send(self, stage, a, kind, src, part):
        step = 1 if kind in (0, 2) else -1
        target = self.block(step, 0) if stage == 1 else self.block(0, step)
        self.copies.send(self.number(stage, a, kind), src, part, target)

    def start(self):
        me = self.part(0, 0, None)
        for stage in (1, 2):
            for kind in (0, 1):
                self.send(stage, 0, kind, self.own, me)

    def got(self, stage, a, kind):
        along = {0: -1, 1: 1, 2: 2, 3: 2}[kind]
        half = {0: None, 1: None, 2: 0, 3: 1}[kind]
        part = self.part(along, 0, half) if stage == 1 else self.part(a, along, half)
        self.copies.arrived(self.number(stage, a, kind), part)

    def onward(self, stage, a, kind):
        along = -1 if kind == 0 else 1
        half = kind
        part = self.part(along, 0, half) if stage == 1 else self.part(a, along, half)
        self.send(stage, a, kind + 2, part, part)

    def second(self, a):
        part = self.part(a, 0, None)
        for kind in (0, 1):
            self.send(2, a, kind, part, part)


def exchange_kernel(owners_hbm, q_hbm, g_hbm, k_hbm, v_hbm, qg_out, k_out, v_out, kvt,
                    owners, q_in, g_in, staging, load_sems, send_sems, recv_sems):
    me = lax.axis_index(MESH_AXIS)
    width = k_out.shape[2]
    loads = [pltpu.make_async_copy(src, dst, load_sems.at[n]) for n, (src, dst) in enumerate((
        (k_hbm, k_out.at[me]), (v_hbm, v_out.at[me]), (q_hbm, q_in), (g_hbm, g_in), (owners_hbm, owners)))]
    for load in loads:
        load.start()
    copies = Copies(send_sems, recv_sems)
    spreads = (Spread(True, k_out.at[me], k_out, copies, 0), Spread(False, v_out.at[me], v_out, copies, 20))
    greet(OFFSETS)
    loads[0].wait()
    loads[1].wait()
    for spread in spreads:
        spread.start()
    loads[2].wait()
    loads[3].wait()
    loads[4].wait()

    def turn(spread, a, b):
        row = 0 if spread.first_is_y else width
        block = spread.block(a, b)
        for h in range(k_out.shape[1] // 128):
            at = pl.ds(pl.multiple_of(block * k_out.shape[1] + h * 128, 128), 128)
            kvt[row:row + width, at] = spread.blocks[block, h * 128:(h + 1) * 128].T

    def slot_for(target):
        slot = jnp.int32(0)
        for s in range(SIDE * SIDE):
            slot = jnp.where(owners[me, s] == target, s, slot)
        return slot

    def reassign(items):
        for n in items:
            target = device_at(*OFFSETS[n])
            slot = slot_for(target)
            staging[n, 0] = q_in[slot]
            staging[n, 1] = g_in[slot]
            copies.send(40 + n, staging.at[n], qg_out.at[:, me], target)

    far = sorted(range(15), key=lambda n: -sum(min(d, SIDE - d) for d in OFFSETS[n]))
    reassign(far[:5])
    for kind in (0, 1):
        for spread in spreads:
            spread.got(1, 0, kind)
            spread.onward(1, 0, kind)
            spread.second(-1 if kind == 0 else 1)
    for spread in spreads:
        for a in (0, -1, 1):
            turn(spread, a, 0)
    reassign(far[5:10])
    for spread in spreads:
        spread.got(1, 0, 2)
        spread.got(1, 0, 3)
        spread.second(2)
    for spread in spreads:
        turn(spread, 2, 0)
    for kind in (0, 1):
        for spread in spreads:
            spread.got(2, 0, kind)
            spread.onward(2, 0, kind)
    reassign(far[10:])
    slot = slot_for(me)
    qg_out[0, me] = q_in[slot]
    qg_out[1, me] = g_in[slot]
    for a in (-1, 1, 2):
        for kind in (0, 1):
            for spread in spreads:
                spread.got(2, a, kind)
                spread.onward(2, a, kind)
    for spread in spreads:
        for a in (0, -1, 1, 2):
            for b in (-1, 1):
                turn(spread, a, b)
    for a in (0, -1, 1, 2):
        for kind in (2, 3):
            for spread in spreads:
                spread.got(2, a, kind)
        for spread in spreads:
            turn(spread, a, 2)

    for n in far:
        dz, dy = OFFSETS[n]
        copies.arrived(40 + n, qg_out.at[:, device_at(-dz, -dy)])
    copies.finish()


def exchange(owners, q, g, k, v):
    shards, rows, width = q.shape
    local = k.shape[0]
    vmem = pl.BlockSpec(memory_space=pltpu.VMEM)
    hbm = pl.BlockSpec(memory_space=pltpu.HBM)
    bf16 = jnp.bfloat16
    return pl.pallas_call(
        exchange_kernel,
        out_shape=(
            jax.ShapeDtypeStruct((2, shards, rows, width), bf16),
            jax.ShapeDtypeStruct((shards, local, width), bf16),
            jax.ShapeDtypeStruct((shards, local, width), bf16),
            jax.ShapeDtypeStruct((2 * width, shards * local), bf16),
        ),
        in_specs=[hbm] * 5,
        out_specs=(vmem, vmem, vmem, vmem),
        scratch_shapes=[
            pltpu.SMEM(owners.shape, jnp.int32),
            pltpu.VMEM((shards, rows, width), bf16),
            pltpu.VMEM((shards, rows, width), bf16),
            pltpu.VMEM((shards - 1, 2, rows, width), bf16),
            pltpu.SemaphoreType.DMA((5,)),
            pltpu.SemaphoreType.DMA((55,)),
            pltpu.SemaphoreType.DMA((55,)),
        ],
        compiler_params=pltpu.CompilerParams(
            collective_id=0, has_side_effects=True, vmem_limit_bytes=24 << 20),
    )(owners, q, g, k, v)


class Collect:
    PLUS, MINUS = (2, 0), (1, 3)

    def __init__(self, first_is_y, blocks, out, copies, base, passing, joined, left, right,
                 sums, own_sum, far2, left2, right2):
        self.first_is_y, self.blocks, self.out, self.copies, self.base = first_is_y, blocks, out, copies, base
        self.passing, self.joined, self.left, self.right = passing, joined, left, right
        self.sums, self.own_sum = sums, own_sum
        self.far2, self.left2, self.right2 = far2, left2, right2

    def device(self, a, b):
        return device_at(b, a) if self.first_is_y else device_at(a, b)

    def begin(self):
        for b in (2, 1, 0, 3):
            step = 1 if b in self.PLUS else -1
            self.copies.send(self.base + b, self.blocks.at[self.device(2, b)], self.passing.at[b],
                             self.device(step, 0))
        for b in (2, 1, 3, 0):
            if b in self.PLUS:
                self.copies.send(self.base + 8 + b, self.blocks.at[self.device(-1, b)],
                                 self.right.at[b], self.device(-1, 0))
            else:
                self.copies.send(self.base + 4 + b, self.blocks.at[self.device(1, b)],
                                 self.left.at[b], self.device(1, 0))

    def join(self, b):
        self.copies.arrived(self.base + b, self.passing.at[b])
        step = 1 if b in self.PLUS else -1
        mine = self.blocks[self.device(step, b)].astype(jnp.float32)
        self.joined[b] = (mine + self.passing[b].astype(jnp.float32)).astype(jnp.bfloat16)
        if step == 1:
            self.copies.send(self.base + 4 + b, self.joined.at[b], self.left.at[b], self.device(1, 0))
        else:
            self.copies.send(self.base + 8 + b, self.joined.at[b], self.right.at[b], self.device(-1, 0))

    def total(self, b):
        self.copies.arrived(self.base + 4 + b, self.left.at[b])
        self.copies.arrived(self.base + 8 + b, self.right.at[b])
        total = (self.blocks[self.device(0, b)].astype(jnp.float32)
                 + self.left[b].astype(jnp.float32) + self.right[b].astype(jnp.float32))
        if b == 0:
            self.own_sum[...] = total
        else:
            self.sums[b] = total.astype(jnp.bfloat16)

    def begin2(self, b):
        land = {1: self.left2, 2: self.far2, 3: self.right2}[b]
        self.copies.send(self.base + 11 + b, self.sums.at[b], land, self.device(0, b))

    def end(self):
        total = self.own_sum[...]
        for b, land in ((1, self.left2), (2, self.far2), (3, self.right2)):
            self.copies.arrived(self.base + 11 + b, land)
            total = total + land[...].astype(jnp.float32)
        self.out[...] = total.astype(jnp.bfloat16)


def collect_kernel(dk_ref, dv_ref, dk_out, dv_out, passing, joined, left, right, sums, own_sum,
                   far2, left2, right2, send_sems, recv_sems):
    copies = Copies(send_sems, recv_sems)
    k_sum, v_sum = [
        Collect(i == 0, blocks, out, copies, 15 * i, passing.at[i], joined.at[i], left.at[i], right.at[i],
                sums.at[i], own_sum.at[i], far2.at[i], left2.at[i], right2.at[i])
        for i, (blocks, out) in enumerate(((dk_ref, dk_out), (dv_ref, dv_out)))]
    both = (k_sum, v_sum)
    greet([(1, 0), (2, 0), (3, 0), (0, 1), (0, 2), (0, 3)])
    for one in both:
        one.begin()
    for b in (2, 1, 0, 3):
        for one in both:
            one.join(b)
    for b in (2, 1, 3):
        for one in both:
            one.total(b)
            one.begin2(b)
    for one in both:
        one.total(0)
    for one in both:
        one.end()
    copies.finish()


def collect(dk, dv):
    shards, local, width = dk.shape
    bf16 = jnp.bfloat16
    vmem = pl.BlockSpec(memory_space=pltpu.VMEM)
    full = (2, SIDE, local, width)
    return pl.pallas_call(
        collect_kernel,
        out_shape=(jax.ShapeDtypeStruct((local, width), bf16),) * 2,
        in_specs=[vmem, vmem],
        out_specs=(vmem, vmem),
        scratch_shapes=[
            pltpu.VMEM(full, bf16), pltpu.VMEM(full, bf16), pltpu.VMEM(full, bf16), pltpu.VMEM(full, bf16),
            pltpu.VMEM(full, bf16), pltpu.VMEM((2, local, width), jnp.float32),
            pltpu.VMEM((2, local, width), bf16), pltpu.VMEM((2, local, width), bf16), pltpu.VMEM((2, local, width), bf16),
            pltpu.SemaphoreType.DMA((30,)),
            pltpu.SemaphoreType.DMA((30,)),
        ],
        compiler_params=pltpu.CompilerParams(
            collective_id=1, has_side_effects=True, vmem_limit_bytes=24 << 20),
    )(dk, dv)


SIZES = (256, 512, 768, 1024, 1536, 2304)
CHUNK = 256


def attention_kernel(scale, me, lengths_hbm, owners_hbm, qg_ref, k_ref, v_ref, kvt,
                     out_hbm, dq_hbm, dk_ref, dv_ref,
                     lengths, owners, load_sems, dk_acc, dv_acc, out_buf, dq_buf, sems, *lanes):
    if me is None:
        me = lax.axis_index("ctx")
    _, shards, rows, width = qg_ref.shape
    keys = k_ref.shape[0]
    ndocs = lengths_hbm.shape[0]
    shard_rows = keys // shards
    block = shard_rows // shards
    heads = rows // block
    per_scale = scale * LOG2E
    f32, bf16 = jnp.float32, jnp.bfloat16
    together = len(lanes) // 3
    lanes = [lanes[3 * n:3 * n + 3] for n in range(together)]

    loads = [pltpu.make_async_copy(src, dst, load_sems.at[n])
             for n, (src, dst) in enumerate(((lengths_hbm, lengths), (owners_hbm, owners)))]
    for load in loads:
        load.start()
    dk_acc[...] = jnp.zeros_like(dk_acc)
    dv_acc[...] = jnp.zeros_like(dv_acc)
    for load in loads:
        load.wait()
    token = lax.broadcasted_iota(jnp.int32, (1, rows), 1) // heads
    key_index = lax.broadcasted_iota(jnp.int32, (CHUNK, rows), 0)

    def copies(j):
        return (pltpu.make_async_copy(out_buf.at[j], out_hbm.at[j], sems.at[0, j]),
                pltpu.make_async_copy(dq_buf.at[j], dq_hbm.at[j], sems.at[1, j]))

    class Segment:
        def __init__(self, j, lane):
            self.j = j
            self.q, self.g = qg_ref.at[0, j], qg_ref.at[1, j]
            self.s_buf, self.d_buf, self.sp_buf = lanes[lane]
            slot = jnp.int32(0)
            for s in range(shards):
                slot = jnp.where(owners[j, s] == me, s, slot)
            first = j * shard_rows + slot * block
            self.pos = first + token
            start = jnp.zeros_like(self.pos)
            low = jnp.int32(0)
            end = jnp.int32(0)
            for d in range(ndocs):
                end = end + lengths[d]
                start = jnp.where(end <= self.pos, end, start)
                low = jnp.where(end <= first, end, low)
            self.start = start
            self.base = (low // 128) * 128
            self.need = first + block - self.base

        def open(self, size):
            self.size = size
            self.at = pl.multiple_of(jnp.minimum(self.base, keys - size), 128)
            self.lower = self.start - self.at
            self.upper = self.pos - self.at
            self.peak = jnp.full((8, rows), NEG, f32)
            self.total = jnp.zeros((8, rows), f32)
            self.dsum = jnp.zeros((8, rows), f32)

        def scores(self, c):
            here = slice(c * CHUNK, (c + 1) * CHUNK)
            span = pl.ds(self.at + c * CHUNK, CHUNK)
            raw = dot(k_ref[span, :], self.q[...], NT)
            self.d_buf[here, :] = dot(v_ref[span, :], self.g[...], NT)
            allowed = (key_index >= self.lower - c * CHUNK) & (key_index <= self.upper - c * CHUNK)
            x = jnp.where(allowed, raw, NEG)
            self.s_buf[here, :] = x
            self.peak = jnp.maximum(self.peak, folded(x, jnp.max))

        def peaked(self):
            self.peak = jnp.max(self.peak, axis=0, keepdims=True)

        def weights(self, c):
            here = slice(c * CHUNK, (c + 1) * CHUNK)
            p = jnp.exp2((self.s_buf[here, :] - self.peak) * per_scale)
            self.s_buf[here, :] = p
            self.total = self.total + folded(p, jnp.sum)
            self.dsum = self.dsum + folded(p * self.d_buf[here, :], jnp.sum)

        def summed(self):
            self.inverse = 1.0 / jnp.sum(self.total, axis=0, keepdims=True)
            self.delta = jnp.sum(self.dsum, axis=0, keepdims=True) * self.inverse

        def slopes(self, c):
            here = slice(c * CHUNK, (c + 1) * CHUNK)
            probs = self.s_buf[here, :] * self.inverse
            slopes = probs * (self.d_buf[here, :] - self.delta)
            slopes, probs = slopes.astype(bf16), probs.astype(bf16)
            self.sp_buf[here, 0:rows] = slopes
            self.sp_buf[here, rows:2 * rows] = probs
            spot = pl.ds(self.at + c * CHUNK, CHUNK)
            dk_acc[spot, :] += dot(slopes, self.q[...], NN)
            dv_acc[spot, :] += dot(probs, self.g[...], NN)

        def finish(self):
            span = pl.ds(self.at, self.size)
            here = slice(0, self.size)
            dq = dot(kvt[0:width, span], self.sp_buf[here, 0:rows], NN)
            out = dot(kvt[width:2 * width, span], self.sp_buf[here, rows:2 * rows], NN)
            dq_buf[self.j] = (dq * scale).T.astype(bf16)
            out_buf[self.j] = out.T.astype(bf16)

    def work(segments, size):
        chunks = range(size // CHUNK)
        for one in segments:
            one.open(size)
        for c in chunks:
            segments[0].scores(c)
        segments[0].peaked()
        if len(segments) == 1:
            for c in chunks:
                segments[0].weights(c)
            segments[0].summed()
            for c in chunks:
                segments[0].slopes(c)
            segments[0].finish()
            return
        for c in chunks:
            segments[0].weights(c)
            segments[1].scores(c)
        segments[0].summed()
        segments[1].peaked()
        for c in chunks:
            segments[0].slopes(c)
            segments[1].weights(c)
        segments[1].summed()
        segments[0].finish()
        for c in chunks:
            segments[1].slopes(c)
        segments[1].finish()

    @pl.loop(0, shards // together)
    def _(n):
        segments = [Segment(n * together + m, m) for m in range(together)]
        need = segments[0].need
        for one in segments[1:]:
            need = jnp.maximum(need, one.need)
        for small, size in zip((0,) + SIZES, SIZES):
            @pl.when((need > small) & (need <= size))
            def _():
                work(segments, size)

        for one in segments:
            for copy in copies(one.j):
                copy.start()

    @pl.loop(0, shards)
    def _(j):
        for s in range(shards):
            rows_at = pl.ds(pl.multiple_of(j * shard_rows + s * block, block), block)
            owner = owners[j, s]
            dk_ref[owner, j] = (dk_acc[rows_at, :] * scale).astype(bf16)
            dv_ref[owner, j] = dv_acc[rows_at, :].astype(bf16)

    @pl.loop(0, shards)
    def _(j):
        for copy in copies(j):
            copy.wait()


def attention(qg, k, v, kvt, lengths, owners, me=None, interpret=False):
    _, shards, rows, width = qg.shape
    local = k.shape[1]
    keys = shards * local
    block = keys // shards // shards
    vmem = pl.BlockSpec(memory_space=pltpu.VMEM)
    hbm = pl.BlockSpec(memory_space=pltpu.HBM)
    f32, bf16 = jnp.float32, jnp.bfloat16
    out, dq, dk, dv = pl.pallas_call(
        functools.partial(attention_kernel, width ** -0.5, me),
        out_shape=(
            jax.ShapeDtypeStruct((shards, rows, width), bf16),
            jax.ShapeDtypeStruct((shards, rows, width), bf16),
            jax.ShapeDtypeStruct((shards, shards, block, width), bf16),
            jax.ShapeDtypeStruct((shards, shards, block, width), bf16),
        ),
        in_specs=[hbm, hbm, vmem, vmem, vmem, vmem],
        out_specs=(hbm, hbm, vmem, vmem),
        scratch_shapes=[
            pltpu.SMEM(lengths.shape, jnp.int32),
            pltpu.SMEM(owners.shape, jnp.int32),
            pltpu.SemaphoreType.DMA((2,)),
            pltpu.VMEM((keys, width), f32),
            pltpu.VMEM((keys, width), f32),
            pltpu.VMEM((shards, rows, width), bf16),
            pltpu.VMEM((shards, rows, width), bf16),
            pltpu.SemaphoreType.DMA((2, shards)),
        ] + 2 * [
            pltpu.VMEM((SIZES[-1], rows), f32),
            pltpu.VMEM((SIZES[-1], rows), f32),
            pltpu.VMEM((SIZES[-1], 2 * rows), bf16),
        ],
        compiler_params=pltpu.CompilerParams(vmem_limit_bytes=40 << 20),
        interpret=interpret,
    )(lengths, owners, qg, k.reshape(keys, width), v.reshape(keys, width), kvt)
    return out, dq, dk.reshape(shards, local, width), dv.reshape(shards, local, width)


def on_device(query, keys, values, output_gradient, doc_lengths, block_owner):
    local, heads, width = query.shape
    shards = SIDE * SIDE
    rows = local // shards * heads
    loaded = (query.reshape(shards, rows, width), output_gradient.reshape(shards, rows, width),
              keys[:, 0], values[:, 0])
    loaded = [pltpu.with_memory_space_constraint(one, pltpu.HBM) for one in loaded]
    lengths, owners = [pltpu.with_memory_space_constraint(one, pltpu.HBM) for one in (doc_lengths, block_owner)]
    qg, k, v, kvt = exchange(owners, *loaded)
    out, dq, dk, dv = attention(qg, k, v, kvt, lengths, owners)
    dk, dv = collect(dk, dv)
    return (
        out.reshape(local, heads, width),
        dq.reshape(local, heads, width),
        dk[:, None],
        dv[:, None],
    )


def solution(mesh):
    rows = P(("dp", "ctx"), "tp", None)
    return jax.shard_map(
        on_device,
        mesh=mesh,
        in_specs=(rows, rows, rows, rows, P("dp"), P("dp", None)),
        out_specs=(rows, rows, rows, rows),
        check_vma=False,
    )
```

```python
import functools

import jax
import jax.numpy as jnp
from jax import lax
from jax.experimental import pallas as pl
from jax.experimental.pallas import tpu as pltpu
from jax.sharding import PartitionSpec as P

NEG = -1e30
LOG2E = 1.4426950408889634
NT = (((1,), (1,)), ((), ()))
NN = (((1,), (0,)), ((), ()))


def dot(a, b, dims):
    return lax.dot_general(a, b, dims, preferred_element_type=jnp.float32)


def folded(x, op):
    return op(x.reshape(x.shape[0] // 8, 8, x.shape[1]), axis=0)


SIDE = 4
MESH_AXIS = "ctx"


def coordinates():
    me = lax.axis_index(MESH_AXIS)
    return lax.div(me, SIDE), lax.rem(me, SIDE)


def device_at(dz, dy):
    z, y = coordinates()
    return lax.rem(z + dz + SIDE, SIDE) * SIDE + lax.rem(y + dy + SIDE, SIDE)


def greet(offsets):
    barrier = pltpu.get_barrier_semaphore()
    for dz, dy in offsets:
        pl.semaphore_signal(barrier, inc=1, device_id={MESH_AXIS: device_at(dz, dy)},
                            device_id_type=pl.DeviceIdType.MESH)
    pl.semaphore_wait(barrier, len(offsets))


class Copies:
    def __init__(self, send_sems, recv_sems):
        self.send_sems, self.recv_sems, self.sent = send_sems, recv_sems, []

    def make(self, n, src, dst, target):
        return pltpu.make_async_remote_copy(
            src_ref=src, dst_ref=dst, send_sem=self.send_sems.at[n], recv_sem=self.recv_sems.at[n],
            device_id={MESH_AXIS: target}, device_id_type=pl.DeviceIdType.MESH)

    def send(self, n, src, dst, target):
        copy = self.make(n, src, dst, target)
        copy.start()
        self.sent.append(copy)

    def arrived(self, n, dst):
        self.make(n, dst, dst, device_at(0, 1)).wait_recv()

    def finish(self):
        for copy in self.sent:
            copy.wait_send()


OFFSETS = [(dz, dy) for dz in (0, 1, 2, 3) for dy in (0, 1, 2, 3) if (dz, dy) != (0, 0)]


class Spread:
    def __init__(self, first_is_y, own, blocks, copies, base):
        self.first_is_y, self.own, self.blocks, self.copies, self.base = first_is_y, own, blocks, copies, base
        self.half = blocks.shape[1] // 2

    def block(self, a, b):
        return device_at(b, a) if self.first_is_y else device_at(a, b)

    def part(self, a, b, half):
        block = self.blocks.at[self.block(a, b)]
        return block if half is None else block.at[pl.ds(half * self.half, self.half)]

    def number(self, stage, a, kind):
        return self.base + (kind if stage == 1 else 4 + 4 * (a % SIDE) + kind)

    def send(self, stage, a, kind, src, part):
        step = 1 if kind in (0, 2) else -1
        target = self.block(step, 0) if stage == 1 else self.block(0, step)
        self.copies.send(self.number(stage, a, kind), src, part, target)

    def start(self):
        me = self.part(0, 0, None)
        for stage in (1, 2):
            for kind in (0, 1):
                self.send(stage, 0, kind, self.own, me)

    def got(self, stage, a, kind):
        along = {0: -1, 1: 1, 2: 2, 3: 2}[kind]
        half = {0: None, 1: None, 2: 0, 3: 1}[kind]
        part = self.part(along, 0, half) if stage == 1 else self.part(a, along, half)
        self.copies.arrived(self.number(stage, a, kind), part)

    def onward(self, stage, a, kind):
        along = -1 if kind == 0 else 1
        half = kind
        part = self.part(along, 0, half) if stage == 1 else self.part(a, along, half)
        self.send(stage, a, kind + 2, part, part)

    def second(self, a):
        part = self.part(a, 0, None)
        for kind in (0, 1):
            self.send(2, a, kind, part, part)


def exchange_kernel(owners_hbm, q_hbm, g_hbm, k_hbm, v_hbm, qg_out, k_out, v_out, kvt,
                    owners, q_in, g_in, staging, load_sems, send_sems, recv_sems):
    me = lax.axis_index(MESH_AXIS)
    width = k_out.shape[2]
    loads = [pltpu.make_async_copy(src, dst, load_sems.at[n]) for n, (src, dst) in enumerate((
        (k_hbm, k_out.at[me]), (v_hbm, v_out.at[me]), (q_hbm, q_in), (g_hbm, g_in), (owners_hbm, owners)))]
    for load in loads:
        load.start()
    copies = Copies(send_sems, recv_sems)
    spreads = (Spread(True, k_hbm, k_out, copies, 0), Spread(False, v_hbm, v_out, copies, 20))
    greet(OFFSETS)
    for spread in spreads:
        spread.start()
    for load in loads:
        load.wait()

    def turn(spread, a, b):
        row = 0 if spread.first_is_y else width
        block = spread.block(a, b)
        for h in range(k_out.shape[1] // 128):
            at = pl.ds(pl.multiple_of(block * k_out.shape[1] + h * 128, 128), 128)
            kvt[row:row + width, at] = spread.blocks[block, h * 128:(h + 1) * 128].T

    def slot_for(target):
        slot = jnp.int32(0)
        for s in range(SIDE * SIDE):
            slot = jnp.where(owners[me, s] == target, s, slot)
        return slot

    def reassign(items):
        for n in items:
            target = device_at(*OFFSETS[n])
            slot = slot_for(target)
            staging[n, 0] = q_in[slot]
            staging[n, 1] = g_in[slot]
            copies.send(40 + n, staging.at[n], qg_out.at[:, me], target)

    far = sorted(range(15), key=lambda n: sum(min(d, SIDE - d) for d in OFFSETS[n]))
    reassign(far[:4])
    for kind in (0, 1):
        for spread in spreads:
            spread.got(1, 0, kind)
            spread.onward(1, 0, kind)
            spread.second(-1 if kind == 0 else 1)
    reassign(far[4:9])
    for spread in spreads:
        spread.got(1, 0, 2)
        spread.got(1, 0, 3)
        spread.second(2)
    for kind in (0, 1):
        for spread in spreads:
            spread.got(2, 0, kind)
            spread.onward(2, 0, kind)
    reassign(far[9:])
    slot = slot_for(me)
    qg_out[0, me] = q_in[slot]
    qg_out[1, me] = g_in[slot]
    for a in (-1, 1, 2):
        for kind in (0, 1):
            for spread in spreads:
                spread.got(2, a, kind)
                spread.onward(2, a, kind)
    for spread in spreads:
        for a in (0, -1, 1, 2):
            for b in (0, -1, 1):
                turn(spread, a, b)
    for a in (0, -1, 1, 2):
        for kind in (2, 3):
            for spread in spreads:
                spread.got(2, a, kind)
        for spread in spreads:
            turn(spread, a, 2)

    for n in far:
        dz, dy = OFFSETS[n]
        copies.arrived(40 + n, qg_out.at[:, device_at(-dz, -dy)])
    copies.finish()


def exchange(owners, q, g, k, v):
    shards, rows, width = q.shape
    local = k.shape[0]
    vmem = pl.BlockSpec(memory_space=pltpu.VMEM)
    hbm = pl.BlockSpec(memory_space=pltpu.HBM)
    bf16 = jnp.bfloat16
    return pl.pallas_call(
        exchange_kernel,
        out_shape=(
            jax.ShapeDtypeStruct((2, shards, rows, width), bf16),
            jax.ShapeDtypeStruct((shards, local, width), bf16),
            jax.ShapeDtypeStruct((shards, local, width), bf16),
            jax.ShapeDtypeStruct((2 * width, shards * local), bf16),
        ),
        in_specs=[hbm] * 5,
        out_specs=(vmem, vmem, vmem, vmem),
        scratch_shapes=[
            pltpu.SMEM(owners.shape, jnp.int32),
            pltpu.VMEM((shards, rows, width), bf16),
            pltpu.VMEM((shards, rows, width), bf16),
            pltpu.VMEM((shards - 1, 2, rows, width), bf16),
            pltpu.SemaphoreType.DMA((5,)),
            pltpu.SemaphoreType.DMA((55,)),
            pltpu.SemaphoreType.DMA((55,)),
        ],
        compiler_params=pltpu.CompilerParams(
            collective_id=0, has_side_effects=True, vmem_limit_bytes=24 << 20),
    )(owners, q, g, k, v)


class Collect:
    PLUS, MINUS = (2, 0), (1, 3)

    def __init__(self, first_is_y, blocks, out, copies, base, passing, joined, left, right,
                 sums, own_sum, far2, left2, right2):
        self.first_is_y, self.blocks, self.out, self.copies, self.base = first_is_y, blocks, out, copies, base
        self.passing, self.joined, self.left, self.right = passing, joined, left, right
        self.sums, self.own_sum = sums, own_sum
        self.far2, self.left2, self.right2 = far2, left2, right2

    def device(self, a, b):
        return device_at(b, a) if self.first_is_y else device_at(a, b)

    def begin(self):
        for b in (2, 1, 0, 3):
            step = 1 if b in self.PLUS else -1
            self.copies.send(self.base + b, self.blocks.at[self.device(2, b)], self.passing.at[b],
                             self.device(step, 0))
        for b in (2, 1, 3, 0):
            if b in self.PLUS:
                self.copies.send(self.base + 8 + b, self.blocks.at[self.device(-1, b)],
                                 self.right.at[b], self.device(-1, 0))
            else:
                self.copies.send(self.base + 4 + b, self.blocks.at[self.device(1, b)],
                                 self.left.at[b], self.device(1, 0))

    def join(self, b):
        self.copies.arrived(self.base + b, self.passing.at[b])
        step = 1 if b in self.PLUS else -1
        mine = self.blocks[self.device(step, b)].astype(jnp.float32)
        self.joined[b] = (mine + self.passing[b].astype(jnp.float32)).astype(jnp.bfloat16)
        if step == 1:
            self.copies.send(self.base + 4 + b, self.joined.at[b], self.left.at[b], self.device(1, 0))
        else:
            self.copies.send(self.base + 8 + b, self.joined.at[b], self.right.at[b], self.device(-1, 0))

    def total(self, b):
        self.copies.arrived(self.base + 4 + b, self.left.at[b])
        self.copies.arrived(self.base + 8 + b, self.right.at[b])
        total = (self.blocks[self.device(0, b)].astype(jnp.float32)
                 + self.left[b].astype(jnp.float32) + self.right[b].astype(jnp.float32))
        if b == 0:
            self.own_sum[...] = total
        else:
            self.sums[b] = total.astype(jnp.bfloat16)

    def begin2(self, b):
        land = {1: self.left2, 2: self.far2, 3: self.right2}[b]
        self.copies.send(self.base + 11 + b, self.sums.at[b], land, self.device(0, b))

    def end(self):
        total = self.own_sum[...]
        for b, land in ((1, self.left2), (2, self.far2), (3, self.right2)):
            self.copies.arrived(self.base + 11 + b, land)
            total = total + land[...].astype(jnp.float32)
        self.out[...] = total.astype(jnp.bfloat16)


def collect_kernel(dk_ref, dv_ref, dk_out, dv_out, passing, joined, left, right, sums, own_sum,
                   far2, left2, right2, send_sems, recv_sems):
    copies = Copies(send_sems, recv_sems)
    k_sum, v_sum = [
        Collect(i == 0, blocks, out, copies, 15 * i, passing.at[i], joined.at[i], left.at[i], right.at[i],
                sums.at[i], own_sum.at[i], far2.at[i], left2.at[i], right2.at[i])
        for i, (blocks, out) in enumerate(((dk_ref, dk_out), (dv_ref, dv_out)))]
    both = (k_sum, v_sum)
    greet([(1, 0), (2, 0), (3, 0), (0, 1), (0, 2), (0, 3)])
    for one in both:
        one.begin()
    for b in (2, 1, 0, 3):
        for one in both:
            one.join(b)
    for b in (2, 1, 3):
        for one in both:
            one.total(b)
            one.begin2(b)
    for one in both:
        one.total(0)
    for one in both:
        one.end()
    copies.finish()


def collect(dk, dv):
    shards, local, width = dk.shape
    bf16 = jnp.bfloat16
    vmem = pl.BlockSpec(memory_space=pltpu.VMEM)
    full = (2, SIDE, local, width)
    return pl.pallas_call(
        collect_kernel,
        out_shape=(jax.ShapeDtypeStruct((local, width), bf16),) * 2,
        in_specs=[vmem, vmem],
        out_specs=(vmem, vmem),
        scratch_shapes=[
            pltpu.VMEM(full, bf16), pltpu.VMEM(full, bf16), pltpu.VMEM(full, bf16), pltpu.VMEM(full, bf16),
            pltpu.VMEM(full, bf16), pltpu.VMEM((2, local, width), jnp.float32),
            pltpu.VMEM((2, local, width), bf16), pltpu.VMEM((2, local, width), bf16), pltpu.VMEM((2, local, width), bf16),
            pltpu.SemaphoreType.DMA((30,)),
            pltpu.SemaphoreType.DMA((30,)),
        ],
        compiler_params=pltpu.CompilerParams(
            collective_id=1, has_side_effects=True, vmem_limit_bytes=24 << 20),
    )(dk, dv)


SIZES = (256, 512, 768, 1024, 1536, 2304)
CHUNK = 256


def attention_kernel(scale, me, lengths_hbm, owners_hbm, qg_ref, k_ref, v_ref, kvt,
                     out_hbm, dq_hbm, dk_ref, dv_ref,
                     lengths, owners, load_sems, dk_acc, dv_acc, out_buf, dq_buf, sems, *lanes):
    if me is None:
        me = lax.axis_index("ctx")
    _, shards, rows, width = qg_ref.shape
    keys = k_ref.shape[0]
    ndocs = lengths_hbm.shape[0]
    shard_rows = keys // shards
    block = shard_rows // shards
    heads = rows // block
    per_scale = scale * LOG2E
    f32, bf16 = jnp.float32, jnp.bfloat16
    together = len(lanes) // 3
    lanes = [lanes[3 * n:3 * n + 3] for n in range(together)]

    loads = [pltpu.make_async_copy(src, dst, load_sems.at[n])
             for n, (src, dst) in enumerate(((lengths_hbm, lengths), (owners_hbm, owners)))]
    for load in loads:
        load.start()
    dk_acc[...] = jnp.zeros_like(dk_acc)
    dv_acc[...] = jnp.zeros_like(dv_acc)
    for load in loads:
        load.wait()
    token = lax.broadcasted_iota(jnp.int32, (1, rows), 1) // heads
    key_index = lax.broadcasted_iota(jnp.int32, (CHUNK, rows), 0)

    def copies(j):
        return (pltpu.make_async_copy(out_buf.at[j], out_hbm.at[j], sems.at[0, j]),
                pltpu.make_async_copy(dq_buf.at[j], dq_hbm.at[j], sems.at[1, j]))

    class Segment:
        def __init__(self, j, lane):
            self.j = j
            self.q, self.g = qg_ref.at[0, j], qg_ref.at[1, j]
            self.s_buf, self.d_buf, self.sp_buf = lanes[lane]
            slot = jnp.int32(0)
            for s in range(shards):
                slot = jnp.where(owners[j, s] == me, s, slot)
            first = j * shard_rows + slot * block
            self.pos = first + token
            start = jnp.zeros_like(self.pos)
            low = jnp.int32(0)
            end = jnp.int32(0)
            for d in range(ndocs):
                end = end + lengths[d]
                start = jnp.where(end <= self.pos, end, start)
                low = jnp.where(end <= first, end, low)
            self.start = start
            self.base = (low // 128) * 128
            self.need = first + block - self.base

        def open(self, size):
            self.size = size
            self.at = pl.multiple_of(jnp.minimum(self.base, keys - size), 128)
            self.lower = self.start - self.at
            self.upper = self.pos - self.at
            self.peak = jnp.full((8, rows), NEG, f32)
            self.total = jnp.zeros((8, rows), f32)
            self.dsum = jnp.zeros((8, rows), f32)

        def scores(self, c):
            here = slice(c * CHUNK, (c + 1) * CHUNK)
            span = pl.ds(self.at + c * CHUNK, CHUNK)
            raw = dot(k_ref[span, :], self.q[...], NT)
            self.d_buf[here, :] = dot(v_ref[span, :], self.g[...], NT)
            allowed = (key_index >= self.lower - c * CHUNK) & (key_index <= self.upper - c * CHUNK)
            x = jnp.where(allowed, raw, NEG)
            self.s_buf[here, :] = x
            self.peak = jnp.maximum(self.peak, folded(x, jnp.max))

        def peaked(self):
            self.peak = jnp.max(self.peak, axis=0, keepdims=True)

        def weights(self, c):
            here = slice(c * CHUNK, (c + 1) * CHUNK)
            p = jnp.exp2((self.s_buf[here, :] - self.peak) * per_scale)
            self.s_buf[here, :] = p
            self.total = self.total + folded(p, jnp.sum)
            self.dsum = self.dsum + folded(p * self.d_buf[here, :], jnp.sum)

        def summed(self):
            self.inverse = 1.0 / jnp.sum(self.total, axis=0, keepdims=True)
            self.delta = jnp.sum(self.dsum, axis=0, keepdims=True) * self.inverse

        def slopes(self, c):
            here = slice(c * CHUNK, (c + 1) * CHUNK)
            probs = self.s_buf[here, :] * self.inverse
            slopes = probs * (self.d_buf[here, :] - self.delta)
            slopes, probs = slopes.astype(bf16), probs.astype(bf16)
            self.sp_buf[here, 0:rows] = slopes
            self.sp_buf[here, rows:2 * rows] = probs
            spot = pl.ds(self.at + c * CHUNK, CHUNK)
            dk_acc[spot, :] += dot(slopes, self.q[...], NN)
            dv_acc[spot, :] += dot(probs, self.g[...], NN)

        def finish(self):
            span = pl.ds(self.at, self.size)
            here = slice(0, self.size)
            dq = dot(kvt[0:width, span], self.sp_buf[here, 0:rows], NN)
            out = dot(kvt[width:2 * width, span], self.sp_buf[here, rows:2 * rows], NN)
            dq_buf[self.j] = (dq * scale).T.astype(bf16)
            out_buf[self.j] = out.T.astype(bf16)

    def work(segments, size):
        chunks = range(size // CHUNK)
        for one in segments:
            one.open(size)
        for c in chunks:
            segments[0].scores(c)
        segments[0].peaked()
        if len(segments) == 1:
            for c in chunks:
                segments[0].weights(c)
            segments[0].summed()
            for c in chunks:
                segments[0].slopes(c)
            segments[0].finish()
            return
        for c in chunks:
            segments[0].weights(c)
            segments[1].scores(c)
        segments[0].summed()
        segments[1].peaked()
        for c in chunks:
            segments[0].slopes(c)
            segments[1].weights(c)
        segments[1].summed()
        segments[0].finish()
        for c in chunks:
            segments[1].slopes(c)
        segments[1].finish()

    @pl.loop(0, shards // together)
    def _(n):
        segments = [Segment(n * together + m, m) for m in range(together)]
        need = segments[0].need
        for one in segments[1:]:
            need = jnp.maximum(need, one.need)
        for small, size in zip((0,) + SIZES, SIZES):
            @pl.when((need > small) & (need <= size))
            def _():
                work(segments, size)

        for one in segments:
            for copy in copies(one.j):
                copy.start()

    @pl.loop(0, shards)
    def _(j):
        for s in range(shards):
            rows_at = pl.ds(pl.multiple_of(j * shard_rows + s * block, block), block)
            owner = owners[j, s]
            dk_ref[owner, j] = (dk_acc[rows_at, :] * scale).astype(bf16)
            dv_ref[owner, j] = dv_acc[rows_at, :].astype(bf16)

    @pl.loop(0, shards)
    def _(j):
        for copy in copies(j):
            copy.wait()


def attention(qg, k, v, kvt, lengths, owners, me=None, interpret=False):
    _, shards, rows, width = qg.shape
    local = k.shape[1]
    keys = shards * local
    block = keys // shards // shards
    vmem = pl.BlockSpec(memory_space=pltpu.VMEM)
    hbm = pl.BlockSpec(memory_space=pltpu.HBM)
    f32, bf16 = jnp.float32, jnp.bfloat16
    out, dq, dk, dv = pl.pallas_call(
        functools.partial(attention_kernel, width ** -0.5, me),
        out_shape=(
            jax.ShapeDtypeStruct((shards, rows, width), bf16),
            jax.ShapeDtypeStruct((shards, rows, width), bf16),
            jax.ShapeDtypeStruct((shards, shards, block, width), bf16),
            jax.ShapeDtypeStruct((shards, shards, block, width), bf16),
        ),
        in_specs=[hbm, hbm, vmem, vmem, vmem, vmem],
        out_specs=(hbm, hbm, vmem, vmem),
        scratch_shapes=[
            pltpu.SMEM(lengths.shape, jnp.int32),
            pltpu.SMEM(owners.shape, jnp.int32),
            pltpu.SemaphoreType.DMA((2,)),
            pltpu.VMEM((keys, width), f32),
            pltpu.VMEM((keys, width), f32),
            pltpu.VMEM((shards, rows, width), bf16),
            pltpu.VMEM((shards, rows, width), bf16),
            pltpu.SemaphoreType.DMA((2, shards)),
        ] + 2 * [
            pltpu.VMEM((SIZES[-1], rows), f32),
            pltpu.VMEM((SIZES[-1], rows), f32),
            pltpu.VMEM((SIZES[-1], 2 * rows), bf16),
        ],
        compiler_params=pltpu.CompilerParams(vmem_limit_bytes=40 << 20),
        interpret=interpret,
    )(lengths, owners, qg, k.reshape(keys, width), v.reshape(keys, width), kvt)
    return out, dq, dk.reshape(shards, local, width), dv.reshape(shards, local, width)


def on_device(query, keys, values, output_gradient, doc_lengths, block_owner):
    local, heads, width = query.shape
    shards = SIDE * SIDE
    rows = local // shards * heads
    loaded = (query.reshape(shards, rows, width), output_gradient.reshape(shards, rows, width),
              keys[:, 0], values[:, 0])
    loaded = [pltpu.with_memory_space_constraint(one, pltpu.HBM) for one in loaded]
    lengths, owners = [pltpu.with_memory_space_constraint(one, pltpu.HBM) for one in (doc_lengths, block_owner)]
    qg, k, v, kvt = exchange(owners, *loaded)
    out, dq, dk, dv = attention(qg, k, v, kvt, lengths, owners)
    dk, dv = collect(dk, dv)
    return (
        out.reshape(local, heads, width),
        dq.reshape(local, heads, width),
        dk[:, None],
        dv[:, None],
    )


def solution(mesh):
    rows = P(("dp", "ctx"), "tp", None)
    return jax.shard_map(
        on_device,
        mesh=mesh,
        in_specs=(rows, rows, rows, rows, P("dp"), P("dp", None)),
        out_specs=(rows, rows, rows, rows),
        check_vma=False,
    )
```

```python
import functools

import jax
import jax.numpy as jnp
from jax import lax
from jax.experimental import pallas as pl
from jax.experimental.pallas import tpu as pltpu
from jax.sharding import PartitionSpec as P

NEG = -1e30
LOG2E = 1.4426950408889634
NT = (((1,), (1,)), ((), ()))
NN = (((1,), (0,)), ((), ()))


def dot(a, b, dims):
    return lax.dot_general(a, b, dims, preferred_element_type=jnp.float32)


def folded(x, op):
    return op(x.reshape(x.shape[0] // 8, 8, x.shape[1]), axis=0)


SIDE = 4
MESH_AXIS = "ctx"


def coordinates():
    me = lax.axis_index(MESH_AXIS)
    return lax.div(me, SIDE), lax.rem(me, SIDE)


def device_at(dz, dy):
    z, y = coordinates()
    return lax.rem(z + dz + SIDE, SIDE) * SIDE + lax.rem(y + dy + SIDE, SIDE)


def greet(offsets):
    barrier = pltpu.get_barrier_semaphore()
    for dz, dy in offsets:
        pl.semaphore_signal(barrier, inc=1, device_id={MESH_AXIS: device_at(dz, dy)},
                            device_id_type=pl.DeviceIdType.MESH)
    pl.semaphore_wait(barrier, len(offsets))


class Copies:
    def __init__(self, send_sems, recv_sems):
        self.send_sems, self.recv_sems, self.sent = send_sems, recv_sems, []

    def make(self, n, src, dst, target):
        return pltpu.make_async_remote_copy(
            src_ref=src, dst_ref=dst, send_sem=self.send_sems.at[n], recv_sem=self.recv_sems.at[n],
            device_id={MESH_AXIS: target}, device_id_type=pl.DeviceIdType.MESH)

    def send(self, n, src, dst, target):
        copy = self.make(n, src, dst, target)
        copy.start()
        self.sent.append(copy)

    def arrived(self, n, dst):
        self.make(n, dst, dst, device_at(0, 1)).wait_recv()

    def finish(self):
        for copy in self.sent:
            copy.wait_send()


OFFSETS = [(dz, dy) for dz in (0, 1, 2, 3) for dy in (0, 1, 2, 3) if (dz, dy) != (0, 0)]


class Spread:
    def __init__(self, first_is_y, own, blocks, copies, base):
        self.first_is_y, self.own, self.blocks, self.copies, self.base = first_is_y, own, blocks, copies, base
        self.half = blocks.shape[1] // 2

    def block(self, a, b):
        return device_at(b, a) if self.first_is_y else device_at(a, b)

    def part(self, a, b, half):
        block = self.blocks.at[self.block(a, b)]
        return block if half is None else block.at[pl.ds(half * self.half, self.half)]

    def number(self, stage, a, kind):
        return self.base + (kind if stage == 1 else 4 + 4 * (a % SIDE) + kind)

    def send(self, stage, a, kind, src, part):
        step = 1 if kind in (0, 2) else -1
        target = self.block(step, 0) if stage == 1 else self.block(0, step)
        self.copies.send(self.number(stage, a, kind), src, part, target)

    def start(self):
        me = self.part(0, 0, None)
        for stage in (1, 2):
            for kind in (0, 1):
                self.send(stage, 0, kind, self.own, me)

    def got(self, stage, a, kind):
        along = {0: -1, 1: 1, 2: 2, 3: 2}[kind]
        half = {0: None, 1: None, 2: 0, 3: 1}[kind]
        part = self.part(along, 0, half) if stage == 1 else self.part(a, along, half)
        self.copies.arrived(self.number(stage, a, kind), part)

    def onward(self, stage, a, kind):
        along = -1 if kind == 0 else 1
        half = kind
        part = self.part(along, 0, half) if stage == 1 else self.part(a, along, half)
        self.send(stage, a, kind + 2, part, part)

    def second(self, a):
        part = self.part(a, 0, None)
        for kind in (0, 1):
            self.send(2, a, kind, part, part)


def exchange_kernel(owners_hbm, q_hbm, g_hbm, k_hbm, v_hbm, qg_out, k_out, v_out, kvt,
                    owners, q_in, g_in, staging, load_sems, send_sems, recv_sems):
    me = lax.axis_index(MESH_AXIS)
    width = k_out.shape[2]
    loads = [pltpu.make_async_copy(src, dst, load_sems.at[n]) for n, (src, dst) in enumerate((
        (k_hbm, k_out.at[me]), (v_hbm, v_out.at[me]), (q_hbm, q_in), (g_hbm, g_in), (owners_hbm, owners)))]
    for load in loads:
        load.start()
    copies = Copies(send_sems, recv_sems)
    spreads = (Spread(True, k_hbm, k_out, copies, 0), Spread(False, v_hbm, v_out, copies, 20))
    greet(OFFSETS)
    for spread in spreads:
        spread.start()
    for load in loads:
        load.wait()

    def turn(spread, a, b):
        row = 0 if spread.first_is_y else width
        block = spread.block(a, b)
        for h in range(k_out.shape[1] // 128):
            at = pl.ds(pl.multiple_of(block * k_out.shape[1] + h * 128, 128), 128)
            kvt[row:row + width, at] = spread.blocks[block, h * 128:(h + 1) * 128].T

    def slot_for(target):
        slot = jnp.int32(0)
        for s in range(SIDE * SIDE):
            slot = jnp.where(owners[me, s] == target, s, slot)
        return slot

    def reassign(items):
        for n in items:
            target = device_at(*OFFSETS[n])
            slot = slot_for(target)
            staging[n, 0] = q_in[slot]
            staging[n, 1] = g_in[slot]
            copies.send(40 + n, staging.at[n], qg_out.at[:, me], target)

    far = sorted(range(15), key=lambda n: sum(min(d, SIDE - d) for d in OFFSETS[n]))
    reassign(far[:4])
    for kind in (0, 1):
        for spread in spreads:
            spread.got(1, 0, kind)
            spread.onward(1, 0, kind)
            spread.second(-1 if kind == 0 else 1)
    reassign(far[4:9])
    for spread in spreads:
        spread.got(1, 0, 2)
        spread.got(1, 0, 3)
        spread.second(2)
    for kind in (0, 1):
        for spread in spreads:
            spread.got(2, 0, kind)
            spread.onward(2, 0, kind)
    reassign(far[9:])
    slot = slot_for(me)
    qg_out[0, me] = q_in[slot]
    qg_out[1, me] = g_in[slot]
    for a in (-1, 1, 2):
        for kind in (0, 1):
            for spread in spreads:
                spread.got(2, a, kind)
                spread.onward(2, a, kind)
    for spread in spreads:
        for a in (0, -1, 1, 2):
            for b in (0, -1, 1):
                turn(spread, a, b)
    for a in (0, -1, 1, 2):
        for kind in (2, 3):
            for spread in spreads:
                spread.got(2, a, kind)
        for spread in spreads:
            turn(spread, a, 2)

    for n in far:
        dz, dy = OFFSETS[n]
        copies.arrived(40 + n, qg_out.at[:, device_at(-dz, -dy)])
    copies.finish()


def exchange(owners, q, g, k, v):
    shards, rows, width = q.shape
    local = k.shape[0]
    vmem = pl.BlockSpec(memory_space=pltpu.VMEM)
    hbm = pl.BlockSpec(memory_space=pltpu.HBM)
    bf16 = jnp.bfloat16
    return pl.pallas_call(
        exchange_kernel,
        out_shape=(
            jax.ShapeDtypeStruct((2, shards, rows, width), bf16),
            jax.ShapeDtypeStruct((shards, local, width), bf16),
            jax.ShapeDtypeStruct((shards, local, width), bf16),
            jax.ShapeDtypeStruct((2 * width, shards * local), bf16),
        ),
        in_specs=[hbm] * 5,
        out_specs=(vmem, vmem, vmem, vmem),
        scratch_shapes=[
            pltpu.SMEM(owners.shape, jnp.int32),
            pltpu.VMEM((shards, rows, width), bf16),
            pltpu.VMEM((shards, rows, width), bf16),
            pltpu.VMEM((shards - 1, 2, rows, width), bf16),
            pltpu.SemaphoreType.DMA((5,)),
            pltpu.SemaphoreType.DMA((55,)),
            pltpu.SemaphoreType.DMA((55,)),
        ],
        compiler_params=pltpu.CompilerParams(
            collective_id=0, has_side_effects=True, vmem_limit_bytes=24 << 20),
    )(owners, q, g, k, v)


class Collect:
    PLUS, MINUS = (2, 0), (1, 3)

    def __init__(self, first_is_y, blocks, out, copies, base, passing, joined, left, right,
                 sums, own_sum, far2, left2, right2):
        self.first_is_y, self.blocks, self.out, self.copies, self.base = first_is_y, blocks, out, copies, base
        self.passing, self.joined, self.left, self.right = passing, joined, left, right
        self.sums, self.own_sum = sums, own_sum
        self.far2, self.left2, self.right2 = far2, left2, right2

    def device(self, a, b):
        return device_at(b, a) if self.first_is_y else device_at(a, b)

    def begin(self):
        for b in (2, 1, 0, 3):
            step = 1 if b in self.PLUS else -1
            self.copies.send(self.base + b, self.blocks.at[self.device(2, b)], self.passing.at[b],
                             self.device(step, 0))
        for b in (2, 1, 3, 0):
            if b in self.PLUS:
                self.copies.send(self.base + 8 + b, self.blocks.at[self.device(-1, b)],
                                 self.right.at[b], self.device(-1, 0))
            else:
                self.copies.send(self.base + 4 + b, self.blocks.at[self.device(1, b)],
                                 self.left.at[b], self.device(1, 0))

    def join(self, b):
        self.copies.arrived(self.base + b, self.passing.at[b])
        step = 1 if b in self.PLUS else -1
        mine = self.blocks[self.device(step, b)].astype(jnp.float32)
        self.joined[b] = (mine + self.passing[b].astype(jnp.float32)).astype(jnp.bfloat16)
        if step == 1:
            self.copies.send(self.base + 4 + b, self.joined.at[b], self.left.at[b], self.device(1, 0))
        else:
            self.copies.send(self.base + 8 + b, self.joined.at[b], self.right.at[b], self.device(-1, 0))

    def total(self, b):
        self.copies.arrived(self.base + 4 + b, self.left.at[b])
        self.copies.arrived(self.base + 8 + b, self.right.at[b])
        total = (self.blocks[self.device(0, b)].astype(jnp.float32)
                 + self.left[b].astype(jnp.float32) + self.right[b].astype(jnp.float32))
        if b == 0:
            self.own_sum[...] = total
        else:
            self.sums[b] = total.astype(jnp.bfloat16)

    def begin2(self, b):
        land = {1: self.left2, 2: self.far2, 3: self.right2}[b]
        self.copies.send(self.base + 11 + b, self.sums.at[b], land, self.device(0, b))

    def end(self):
        total = self.own_sum[...]
        for b, land in ((1, self.left2), (2, self.far2), (3, self.right2)):
            self.copies.arrived(self.base + 11 + b, land)
            total = total + land[...].astype(jnp.float32)
        self.out[...] = total.astype(jnp.bfloat16)


def collect_kernel(dk_ref, dv_ref, dk_out, dv_out, passing, joined, left, right, sums, own_sum,
                   far2, left2, right2, send_sems, recv_sems):
    copies = Copies(send_sems, recv_sems)
    k_sum, v_sum = [
        Collect(i == 0, blocks, out, copies, 15 * i, passing.at[i], joined.at[i], left.at[i], right.at[i],
                sums.at[i], own_sum.at[i], far2.at[i], left2.at[i], right2.at[i])
        for i, (blocks, out) in enumerate(((dk_ref, dk_out), (dv_ref, dv_out)))]
    both = (k_sum, v_sum)
    greet([(1, 0), (2, 0), (3, 0), (0, 1), (0, 2), (0, 3)])
    for one in both:
        one.begin()
    for b in (2, 1, 0, 3):
        for one in both:
            one.join(b)
    for b in (2, 1, 3):
        for one in both:
            one.total(b)
            one.begin2(b)
    for one in both:
        one.total(0)
    for one in both:
        one.end()
    copies.finish()


def collect(dk, dv):
    shards, local, width = dk.shape
    bf16 = jnp.bfloat16
    vmem = pl.BlockSpec(memory_space=pltpu.VMEM)
    full = (2, SIDE, local, width)
    return pl.pallas_call(
        collect_kernel,
        out_shape=(jax.ShapeDtypeStruct((local, width), bf16),) * 2,
        in_specs=[vmem, vmem],
        out_specs=(vmem, vmem),
        scratch_shapes=[
            pltpu.VMEM(full, bf16), pltpu.VMEM(full, bf16), pltpu.VMEM(full, bf16), pltpu.VMEM(full, bf16),
            pltpu.VMEM(full, bf16), pltpu.VMEM((2, local, width), jnp.float32),
            pltpu.VMEM((2, local, width), bf16), pltpu.VMEM((2, local, width), bf16), pltpu.VMEM((2, local, width), bf16),
            pltpu.SemaphoreType.DMA((30,)),
            pltpu.SemaphoreType.DMA((30,)),
        ],
        compiler_params=pltpu.CompilerParams(
            collective_id=1, has_side_effects=True, vmem_limit_bytes=24 << 20),
    )(dk, dv)


SIZES = (256, 512, 768, 1024, 1536, 2304)
CHUNK = 256


def attention_kernel(scale, me, lengths_hbm, owners_hbm, qg_ref, k_ref, v_ref, kvt,
                     out_hbm, dq_hbm, dk_ref, dv_ref,
                     lengths, owners, load_sems, dk_acc, dv_acc, out_buf, dq_buf, sems, *lanes):
    if me is None:
        me = lax.axis_index("ctx")
    _, shards, rows, width = qg_ref.shape
    keys = k_ref.shape[0]
    ndocs = lengths_hbm.shape[0]
    shard_rows = keys // shards
    block = shard_rows // shards
    heads = rows // block
    per_scale = scale * LOG2E
    f32, bf16 = jnp.float32, jnp.bfloat16
    together = len(lanes) // 3
    lanes = [lanes[3 * n:3 * n + 3] for n in range(together)]

    loads = [pltpu.make_async_copy(src, dst, load_sems.at[n])
             for n, (src, dst) in enumerate(((lengths_hbm, lengths), (owners_hbm, owners)))]
    for load in loads:
        load.start()
    dk_acc[...] = jnp.zeros_like(dk_acc)
    dv_acc[...] = jnp.zeros_like(dv_acc)
    for load in loads:
        load.wait()
    token = lax.broadcasted_iota(jnp.int32, (1, rows), 1) // heads
    key_index = lax.broadcasted_iota(jnp.int32, (CHUNK, rows), 0)

    def copies(j):
        return (pltpu.make_async_copy(out_buf.at[j], out_hbm.at[j], sems.at[0, j]),
                pltpu.make_async_copy(dq_buf.at[j], dq_hbm.at[j], sems.at[1, j]))

    class Segment:
        def __init__(self, j, lane):
            self.j = j
            self.q, self.g = qg_ref.at[0, j], qg_ref.at[1, j]
            self.s_buf, self.d_buf, self.sp_buf = lanes[lane]
            slot = jnp.int32(0)
            for s in range(shards):
                slot = jnp.where(owners[j, s] == me, s, slot)
            first = j * shard_rows + slot * block
            self.pos = first + token
            start = jnp.zeros_like(self.pos)
            low = jnp.int32(0)
            end = jnp.int32(0)
            for d in range(ndocs):
                end = end + lengths[d]
                start = jnp.where(end <= self.pos, end, start)
                low = jnp.where(end <= first, end, low)
            self.start = start
            self.base = (low // 128) * 128
            self.need = first + block - self.base

        def open(self, size):
            self.size = size
            self.at = pl.multiple_of(jnp.minimum(self.base, keys - size), 128)
            self.lower = self.start - self.at
            self.upper = self.pos - self.at
            self.peak = jnp.full((8, rows), NEG, f32)
            self.total = jnp.zeros((8, rows), f32)
            self.dsum = jnp.zeros((8, rows), f32)

        def scores(self, c):
            here = slice(c * CHUNK, (c + 1) * CHUNK)
            span = pl.ds(self.at + c * CHUNK, CHUNK)
            raw = dot(k_ref[span, :], self.q[...], NT)
            self.d_buf[here, :] = dot(v_ref[span, :], self.g[...], NT)
            allowed = (key_index - (self.lower - c * CHUNK)).astype(jnp.uint32) <= (self.upper - self.lower).astype(jnp.uint32)
            x = jnp.where(allowed, raw, NEG)
            self.s_buf[here, :] = x
            self.peak = jnp.maximum(self.peak, folded(x, jnp.max))

        def peaked(self):
            self.peak = jnp.max(self.peak, axis=0, keepdims=True)

        def weights(self, c):
            here = slice(c * CHUNK, (c + 1) * CHUNK)
            p = jnp.exp2((self.s_buf[here, :] - self.peak) * per_scale)
            self.s_buf[here, :] = p
            self.total = self.total + folded(p, jnp.sum)
            self.dsum = self.dsum + folded(p * self.d_buf[here, :], jnp.sum)

        def summed(self):
            self.inverse = 1.0 / jnp.sum(self.total, axis=0, keepdims=True)
            self.delta = jnp.sum(self.dsum, axis=0, keepdims=True) * self.inverse

        def slopes(self, c):
            here = slice(c * CHUNK, (c + 1) * CHUNK)
            probs = self.s_buf[here, :] * self.inverse
            slopes = probs * (self.d_buf[here, :] - self.delta)
            slopes, probs = slopes.astype(bf16), probs.astype(bf16)
            self.sp_buf[here, 0:rows] = slopes
            self.sp_buf[here, rows:2 * rows] = probs
            spot = pl.ds(self.at + c * CHUNK, CHUNK)
            dk_acc[spot, :] += dot(slopes, self.q[...], NN)
            dv_acc[spot, :] += dot(probs, self.g[...], NN)

        def finish(self):
            span = pl.ds(self.at, self.size)
            here = slice(0, self.size)
            dq = dot(kvt[0:width, span], self.sp_buf[here, 0:rows], NN)
            out = dot(kvt[width:2 * width, span], self.sp_buf[here, rows:2 * rows], NN)
            dq_buf[self.j] = (dq * scale).T.astype(bf16)
            out_buf[self.j] = out.T.astype(bf16)

    def work(segments, size):
        chunks = range(size // CHUNK)
        for one in segments:
            one.open(size)
        for c in chunks:
            segments[0].scores(c)
        segments[0].peaked()
        if len(segments) == 1:
            for c in chunks:
                segments[0].weights(c)
            segments[0].summed()
            for c in chunks:
                segments[0].slopes(c)
            segments[0].finish()
            return
        for c in chunks:
            segments[0].weights(c)
            segments[1].scores(c)
        segments[0].summed()
        segments[1].peaked()
        for c in chunks:
            segments[0].slopes(c)
            segments[1].weights(c)
        segments[1].summed()
        segments[0].finish()
        for c in chunks:
            segments[1].slopes(c)
        segments[1].finish()

    @pl.loop(0, shards // together)
    def _(n):
        segments = [Segment(n * together + m, m) for m in range(together)]
        need = segments[0].need
        for one in segments[1:]:
            need = jnp.maximum(need, one.need)
        for small, size in zip((0,) + SIZES, SIZES):
            @pl.when((need > small) & (need <= size))
            def _():
                work(segments, size)

        for one in segments:
            for copy in copies(one.j):
                copy.start()

    @pl.loop(0, shards)
    def _(j):
        for s in range(shards):
            rows_at = pl.ds(pl.multiple_of(j * shard_rows + s * block, block), block)
            owner = owners[j, s]
            dk_ref[owner, j] = (dk_acc[rows_at, :] * scale).astype(bf16)
            dv_ref[owner, j] = dv_acc[rows_at, :].astype(bf16)

    @pl.loop(0, shards)
    def _(j):
        for copy in copies(j):
            copy.wait()


def attention(qg, k, v, kvt, lengths, owners, me=None, interpret=False):
    _, shards, rows, width = qg.shape
    local = k.shape[1]
    keys = shards * local
    block = keys // shards // shards
    vmem = pl.BlockSpec(memory_space=pltpu.VMEM)
    hbm = pl.BlockSpec(memory_space=pltpu.HBM)
    f32, bf16 = jnp.float32, jnp.bfloat16
    out, dq, dk, dv = pl.pallas_call(
        functools.partial(attention_kernel, width ** -0.5, me),
        out_shape=(
            jax.ShapeDtypeStruct((shards, rows, width), bf16),
            jax.ShapeDtypeStruct((shards, rows, width), bf16),
            jax.ShapeDtypeStruct((shards, shards, block, width), bf16),
            jax.ShapeDtypeStruct((shards, shards, block, width), bf16),
        ),
        in_specs=[hbm, hbm, vmem, vmem, vmem, vmem],
        out_specs=(hbm, hbm, vmem, vmem),
        scratch_shapes=[
            pltpu.SMEM(lengths.shape, jnp.int32),
            pltpu.SMEM(owners.shape, jnp.int32),
            pltpu.SemaphoreType.DMA((2,)),
            pltpu.VMEM((keys, width), f32),
            pltpu.VMEM((keys, width), f32),
            pltpu.VMEM((shards, rows, width), bf16),
            pltpu.VMEM((shards, rows, width), bf16),
            pltpu.SemaphoreType.DMA((2, shards)),
        ] + 2 * [
            pltpu.VMEM((SIZES[-1], rows), f32),
            pltpu.VMEM((SIZES[-1], rows), f32),
            pltpu.VMEM((SIZES[-1], 2 * rows), bf16),
        ],
        compiler_params=pltpu.CompilerParams(vmem_limit_bytes=40 << 20),
        interpret=interpret,
    )(lengths, owners, qg, k.reshape(keys, width), v.reshape(keys, width), kvt)
    return out, dq, dk.reshape(shards, local, width), dv.reshape(shards, local, width)


def on_device(query, keys, values, output_gradient, doc_lengths, block_owner):
    local, heads, width = query.shape
    shards = SIDE * SIDE
    rows = local // shards * heads
    loaded = (query.reshape(shards, rows, width), output_gradient.reshape(shards, rows, width),
              keys[:, 0], values[:, 0])
    loaded = [pltpu.with_memory_space_constraint(one, pltpu.HBM) for one in loaded]
    lengths, owners = [pltpu.with_memory_space_constraint(one, pltpu.HBM) for one in (doc_lengths, block_owner)]
    qg, k, v, kvt = exchange(owners, *loaded)
    out, dq, dk, dv = attention(qg, k, v, kvt, lengths, owners)
    dk, dv = collect(dk, dv)
    return (
        out.reshape(local, heads, width),
        dq.reshape(local, heads, width),
        dk[:, None],
        dv[:, None],
    )


def solution(mesh):
    rows = P(("dp", "ctx"), "tp", None)
    return jax.shard_map(
        on_device,
        mesh=mesh,
        in_specs=(rows, rows, rows, rows, P("dp"), P("dp", None)),
        out_specs=(rows, rows, rows, rows),
        check_vma=False,
    )
```
